32 devices in a mesh: groups: 2 (over y), seq: 4 (over z), heads: 2 (over x), sub: 2 (over core).
Axes of the slice: x: 2, y: 2, z: 4, core: 2. Of those that a mesh axis runs over, the one named last changes fastest.
Arguments:
- queries: bfloat16 [4096, 2048], P(('groups', 'seq', 'heads', 'sub')), parts along dimension 0, may hold values from -12.5 to 12.5
- new_keys: bfloat16 [4096, 2048], P(('groups', 'seq', 'heads', 'sub')), parts along dimension 0, may hold values from -5 to 5
- new_values: bfloat16 [4096, 2048], P(('groups', 'seq', 'heads', 'sub')), parts along dimension 0, may hold values from -5 to 5
- cache_keys: bfloat16 [8192, 2048], P(('groups', 'seq'), ('heads', 'sub')), parts along dimension 0, may hold values from -5 to 5
- cache_values: bfloat16 [8192, 2048], P(('groups', 'seq'), ('heads', 'sub')), parts along dimension 0, may hold values from -5 to 5
- selection: int32 [8, 16, 8], P(('groups', 'seq'), ('heads', 'sub')), parts along dimension 0, may hold values from 0 to 7, as said below
Outputs:
- attended: bfloat16 [4096, 2048], P(('groups', 'seq', 'heads', 'sub')), parts along dimension 0
The draws below stay inside these ranges and needn't reach their ends.
There are 2 independent parts, one for each index of `groups`. The reference program is written for one: setup_inputs(seed, part) draws one part's arguments, and reference() takes and returns one part's arrays. A program takes and returns all parts, laid end to end along the dimension named above; each array names one. Nothing has to cross between parts.
Inputs may be any that keep to these rules, and one draw needn't show every extreme that they name: `selection`: every selected block precedes the span; the 8 blocks of one query block and head are different. For one index of seq and one index of heads+sub, of the 32 selections of that device's query blocks and heads (heads taken in order from index times 4), exactly 8 names a block held by each index of seq (blocks index * 2 to index * 2 + 1).
All inputs are finite; a program needn't handle non-finite values.
Results may differ from the reference program's by a relative error of at most 0.0023.
Values may be sent and summed in bfloat16 or wider, within the bound.
A program may use at most 128 MiB of HBM per device.

```python
import jax
import jax.numpy as jnp
from jax import lax

HD = 128
HEAD_DEV = 4
BLOCK = 512
TOPK = 8
QB_DEV = 1
CB_DEV = 2
HEADS = 16
WIDTH = 2048
QBLK = 4
QTOK = 2048
NCB = 8
CTX = 4096
N_SEQ = 4


def draw_queries(key, part):
    noise_key = jax.random.fold_in(key, 1)
    values = jnp.clip(2.5 * jax.random.normal(noise_key, (QTOK, HEADS * HD), jnp.float32), -12.5, 12.5)
    return values.astype(jnp.bfloat16)


def draw_new_keys(key, part):
    noise_key = jax.random.fold_in(key, 2)
    values = jnp.clip(jax.random.normal(noise_key, (QTOK, HEADS * HD), jnp.float32), -5.0, 5.0)
    return values.astype(jnp.bfloat16)


def draw_selection(key, part):
    group_count = HEADS // HEAD_DEV
    request_count = QB_DEV * HEAD_DEV * TOPK
    keys = jax.random.split(jax.random.fold_in(key, 3), N_SEQ * group_count)

    def one_group(group_key):
        first_key, second_key = jax.random.split(group_key)
        shuffled = jax.random.permutation(first_key, N_SEQ)
        offsets = jax.random.randint(second_key, (N_SEQ,), 0, CB_DEV)
        counter = jnp.arange(request_count)
        source = shuffled[counter % N_SEQ]
        inner = (counter // N_SEQ + offsets[source]) % CB_DEV
        return (source * CB_DEV + inner).astype(jnp.int32)
    flat = jax.vmap(one_group)(keys)
    shaped = flat.reshape(N_SEQ, group_count, QB_DEV, HEAD_DEV, TOPK)
    return shaped.transpose(0, 2, 1, 3, 4).reshape(N_SEQ * QB_DEV, HEADS, TOPK)


def shard_levels(rng, dims, cuts, least, high):
    factor_of = 1.0
    for axis_at, blocks in cuts:
        draws = jax.random.uniform(jax.random.fold_in(jax.random.fold_in(rng, 6), axis_at), (blocks,), jnp.float32, least / len(cuts), high / len(cuts))
        factor_of = factor_of * jnp.repeat(jnp.exp(draws), dims[axis_at] // blocks).reshape((-1,) + (1,) * (len(dims) - 1 - axis_at))
    return factor_of


def scatter_about(own_key, shape, scale, most, shards=(), held_as=jnp.bfloat16):
    drawn = jax.random.normal(own_key, shape, jnp.float32) * scale
    if len(shards) > 0:
        drawn = shard_levels(own_key, shape, shards, -0.22, 0.18) * drawn
    return jnp.clip(drawn, min=-most, max=most).astype(held_as)


def setup_inputs(seed: int = 0, part: int = 0) -> dict:
    key_of = jax.random.split(jax.random.key(seed), 7)
    part_keys = jax.random.split(jax.random.fold_in(key_of[6], part), 7)
    queries = draw_queries(jax.random.fold_in(jax.random.fold_in(key_of[6], part), 71), part)
    new_keys = draw_new_keys(jax.random.fold_in(jax.random.fold_in(key_of[6], part), 71), part)
    new_values = scatter_about(part_keys[2], (QTOK, WIDTH), 1.0, 5.0, ((0, 16),))
    cache_keys = scatter_about(part_keys[3], (CTX, WIDTH), 1.0, 5.0, ((0, 4), (1, 4)))
    cache_values = scatter_about(part_keys[4], (CTX, WIDTH), 1.0, 5.0, ((0, 4), (1, 4)))
    selection = draw_selection(jax.random.fold_in(jax.random.fold_in(key_of[6], part), 71), part)
    return {"queries": queries, "new_keys": new_keys, "new_values": new_values, "cache_keys": cache_keys, "cache_values": cache_values, "selection": selection}


def attend(query_heads, key_heads, value_heads, causal, scaling):
    scores = jnp.einsum("hqd,hkd->hqk", query_heads.astype(jnp.float32), key_heads.astype(jnp.float32)) * scaling
    if causal is not None:
        scores = jnp.where(causal[None, :, :], scores, -jnp.inf)
    highest = jnp.max(scores, axis=-1)
    weights = jnp.exp(scores - highest[..., None])
    totals = jnp.sum(weights, axis=-1)
    rounded = lax.optimization_barrier(weights.astype(jnp.bfloat16)).astype(jnp.float32)
    mixed = jnp.einsum("hqk,hkd->hqd", rounded, value_heads.astype(jnp.float32))
    return mixed, highest, totals


def reference(queries, new_keys, new_values, cache_keys, cache_values, selection):
    scaling = HD ** -0.5
    cache_k = cache_keys.reshape(NCB, BLOCK, HEADS, HD)
    cache_v = cache_values.reshape(NCB, BLOCK, HEADS, HD)
    head_index = jnp.arange(HEADS).astype(jnp.int32)[:, None]
    causal = jnp.arange(BLOCK)[:, None] >= jnp.arange(BLOCK)[None, :]

    def one_block(position):
        begin = (position * BLOCK).astype(jnp.int32)

        def heads_of(array):
            rows = lax.dynamic_slice_in_dim(array, begin, BLOCK, 0)
            return rows.reshape(BLOCK, HEADS, HD).transpose(1, 0, 2)

        query_heads = heads_of(queries)
        chosen = lax.dynamic_index_in_dim(selection, position, 0, keepdims=False).astype(jnp.int32)
        chosen_k = cache_k[chosen, :, head_index, :]
        chosen_v = cache_v[chosen, :, head_index, :]
        parts = [attend(query_heads, heads_of(new_keys), heads_of(new_values), causal, scaling)]
        for turn in range(TOPK):
            parts.append(attend(query_heads, chosen_k[:, turn], chosen_v[:, turn], None, scaling))
        top = parts[0][1]
        for part in parts[1:]:
            top = jnp.maximum(top, part[1])
        numer = jnp.zeros((HEADS, BLOCK, HD), jnp.float32)
        denom = jnp.zeros((HEADS, BLOCK), jnp.float32)
        for part in parts:
            factor = jnp.exp(part[1] - top)
            numer = numer + factor[..., None] * part[0]
            denom = denom + factor * part[2]
        result = numer / denom[..., None]
        return result.transpose(1, 0, 2).reshape(BLOCK, HEADS * HD).astype(jnp.bfloat16)

    blocks_out = lax.map(one_block, jnp.arange(QBLK).astype(jnp.int32))
    return blocks_out.reshape(QTOK, HEADS * HD)
```

```python
import functools
import heapq
import math

import jax
import jax.numpy as jnp
from jax import lax
from jax.experimental import pallas as pl
from jax.experimental.pallas import tpu as pltpu
from jax.sharding import PartitionSpec as P

HD = 128
BLOCK = 512


MESH = pl.DeviceIdType.MESH
TILE = 256

READY, PASS, TAKE, WORK, LOAD, OWN, FOLD, EMIT, DONE, REST = range(10)
KINDS = 16
SEND, UNIT, SPAN, MERGE, CLOSE, WIRE, HOP = 0.06, 1.0, 0.45, 0.3, 0.4, 1.43, 2.0
FIRST, EACH, LATE, DEEP = 2.0, 0.7, 21.0, 2


def plan_steps(count, chunks):
    steps = [[] for _ in range(count)]
    free = [0.0] * count
    seen, back = ([{} for _ in range(count)] for _ in range(2))
    touched, passed, worked, owned, folded, emitted, finished = (
        [set() for _ in range(count)] for _ in range(7)
    )
    wires = {(s, d): [] for s in range(count) for d in (-1, 1) if 0 <= s + d < count}
    heap = []
    for s in range(count):
        for n in range(chunks):
            seen[s][s, n] = FIRST + EACH * n
            heapq.heappush(heap, (seen[s][s, n], s))
        heapq.heappush(heap, (LATE, s))

    def first_use(s, o, n):
        if (o, n) not in touched[s]:
            touched[s].add((o, n))
            steps[s].append((READY if o == s else TAKE, o, n, 0))

    def launch(t, s, d, arrive, entry):
        finish = max([t] + wires[s, d][-1:]) + WIRE
        wires[s, d].append(finish)
        arrive[s + d][entry] = finish + HOP
        heapq.heappush(heap, (finish + HOP, s + d))
        heapq.heappush(heap, (finish, s))

    def next_send(t, s, d):
        found = []
        for (o, n), when in seen[s].items():
            onward = o == s or (o < s) == (d > 0)
            if when <= t and onward and (o, n, d) not in passed[s]:
                left = count - 1 - s if d > 0 else s
                found.append((n - left + (3.0 if o == s else 0.0), 0, o, n))
        for o, n in folded[s]:
            if (o - s) * d > 0 and (o, n) not in emitted[s]:
                found.append((n + 8.0 - 2.0 * abs(o - s), 1, o, n))
        return min(found) if found else None

    def next_work(t, s):
        found = []
        for o, n in worked[s]:
            if o != s and (o, n) not in folded[s]:
                far = s + (s - o) // abs(s - o)
                if not 0 <= far < count or back[s].get((o, n), t + 1) <= t:
                    found.append((0, n - 2 * abs(o - s), FOLD, o, n, MERGE))
        for n in range(chunks):
            if (s, n) in worked[s] and n in owned[s] and n not in finished[s]:
                sides = [d for d in (-1, 1) if (s, d) in wires]
                if all(back[s].get((s, n, d), t + 1) <= t for d in sides):
                    found.append((1, n, DONE, s, n, CLOSE))
        for (o, n), when in seen[s].items():
            if when <= t and (o, n) not in worked[s]:
                found.append((2, n - abs(o - s), WORK, o, n, UNIT))
        if t >= LATE:
            for n in range(chunks):
                if n not in owned[s] and (s, n) in worked[s]:
                    found.append((2, n + 3.5, OWN, s, n, SPAN))
        return min(found) if found else None

    while heap:
        t, s = heapq.heappop(heap)
        if t < free[s] - 1e-9:
            continue
        for d in (-1, 1):
            while (s, d) in wires and sum(f > t for f in wires[s, d]) < DEEP:
                best = next_send(t, s, d)
                if best is None:
                    break
                _, out, o, n = best
                if out:
                    emitted[s].add((o, n))
                    steps[s].append((EMIT, o, n, d))
                    launch(t, s, d, back, (o, n, -d) if s + d == o else (o, n))
                else:
                    first_use(s, o, n)
                    passed[s].add((o, n, d))
                    steps[s].append((PASS, o, n, d))
                    launch(t, s, d, seen, (o, n))
                t += SEND
        best = next_work(t, s)
        free[s] = t
        if best is None:
            continue
        _, _, kind, o, n, price = best
        if kind == WORK:
            first_use(s, o, n)
            worked[s].add((o, n))
        elif kind == OWN:
            if not owned[s]:
                steps[s].append((LOAD, o, n, 0))
            owned[s].add(n)
        elif kind == FOLD:
            folded[s].add((o, n))
        else:
            finished[s].add(n)
        steps[s].append((kind, o, n, 0))
        free[s] = t + price
        heapq.heappush(heap, (free[s], s))
    return steps


def plan_codes(count, chunks):
    steps = plan_steps(count, chunks)
    codes = []
    for s, one in enumerate(steps):
        row = [
            k + KINDS * ((d > 0) + 2 * (o + count * n))
            for k, o, n, d in one
            if not (o == s and n == 0 and k in (READY, PASS))
        ]
        codes.append(row)
    base = KINDS * 2 * count * chunks
    each = max(k for k in range(1, 8) if base**k < 2**31)
    longest = -(-max(len(row) for row in codes) // each)
    words = []
    for row in codes:
        row = row + [REST] * (longest * each - len(row))
        words.append(
            [sum(row[w * each + k] * base**k for k in range(each)) for w in range(longest)]
        )
    return words, base, each


def pick_word(words, index):
    if len(words) == 1:
        return words[0]
    half = 1 << (len(words) - 1).bit_length() - 1
    low, high = words[:half], words[half:]
    return jnp.where(index >= half, pick_word(high, index - half), pick_word(low, index))


def span_tile(rows, length):
    return min(length, max(rows, TILE))


def columns(head):
    return pl.ds(pl.multiple_of(head * HD, HD), HD)


def fused_kernel(
    seq_count, heads_size, sub_size, head_count,
    q_ref, k_ref, v_ref, ck_ref, cv_ref, out_ref,
    qall, kown, vown, kc, vc, vt, msg_in, st_in, msg_out, st_out, part, pst, fin,
    loc_sem, xq_send, xq_recv, xkv_send, xkv_recv, zq_send, zq_recv,
    m_send, m_recv, t_send, t_recv, o_send, o_recv, o_loc,
):
    peers = heads_size * sub_size
    rows, span_cols = q_ref.shape[0], head_count * HD
    length = rows * peers
    tile = span_tile(rows, length)
    halves, bands = length // tile, tile // rows
    chunks = head_count * halves
    cache_blocks = kc.shape[0] // BLOCK
    scaling = HD ** (-0.5) * math.log2(math.e)
    at_seq = lax.axis_index("seq")
    place = lax.axis_index("heads") * sub_size + lax.axis_index("sub")
    has_left, has_right = at_seq > 0, at_seq < seq_count - 1

    def peer_of(step):
        return lax.rem(place + step, peers)

    def peer_id(peer):
        return {"heads": peer // sub_size, "sub": lax.rem(peer, sub_size)}

    def band(index):
        return pl.ds(pl.multiple_of(index * rows, rows), rows)

    def slab(index):
        return pl.ds(pl.multiple_of(index * span_cols, span_cols), span_cols)

    def head_cols(peer, head):
        return pl.ds(pl.multiple_of(peer * span_cols + head * HD, HD), HD)

    barrier = pltpu.get_barrier_semaphore()
    for step in range(1, peers):
        pl.semaphore_signal(barrier, inc=1, device_id=peer_id(peer_of(step)), device_id_type=MESH)

    @pl.when(has_left)
    def _():
        pl.semaphore_signal(barrier, inc=1, device_id={"seq": at_seq - 1}, device_id_type=MESH)

    @pl.when(has_right)
    def _():
        pl.semaphore_signal(barrier, inc=1, device_id={"seq": at_seq + 1}, device_id_type=MESH)

    own = [
        pltpu.make_async_copy(
            q_ref.at[:, slab(place)], qall.at[at_seq, band(place), :], loc_sem.at[0]
        ),
        pltpu.make_async_copy(k_ref.at[:, slab(place)], kown.at[band(place), :], loc_sem.at[1]),
        pltpu.make_async_copy(v_ref.at[:, slab(place)], vown.at[band(place), :], loc_sem.at[2]),
        pltpu.make_async_copy(ck_ref, kc, loc_sem.at[3]),
        pltpu.make_async_copy(cv_ref, vc, loc_sem.at[4]),
    ]
    for copy in (own[0], own[4], own[3], own[1], own[2]):
        copy.start()
    plans, base, each = plan_codes(seq_count, chunks)
    words = []
    for index in range(len(plans[0])):
        value = jnp.int32(plans[0][index])
        for s in range(1, seq_count):
            value = jnp.where(at_seq == s, jnp.int32(plans[s][index]), value)
        words.append(value)
    sides = has_left.astype(jnp.int32) + has_right.astype(jnp.int32)
    pl.semaphore_wait(barrier, peers - 1 + sides)

    def spread_q(peer, head):
        return pltpu.make_async_remote_copy(
            src_ref=q_ref.at[:, head_cols(peer, head)],
            dst_ref=qall.at[at_seq, band(place), columns(head)],
            send_sem=xq_send.at[head, peer],
            recv_sem=xq_recv.at[head, place],
            device_id=peer_id(peer),
            device_id_type=MESH,
        )

    def landed_q(peer, head):
        return pltpu.make_async_remote_copy(
            src_ref=q_ref.at[:, head_cols(peer, head)],
            dst_ref=qall.at[at_seq, band(peer), columns(head)],
            send_sem=xq_send.at[head, peer],
            recv_sem=xq_recv.at[head, peer],
            device_id=peer_id(peer),
            device_id_type=MESH,
        )

    def spread_kv(which, peer, source):
        ref, buffer = ((k_ref, kown), (v_ref, vown))[which]
        return pltpu.make_async_remote_copy(
            src_ref=ref.at[:, slab(peer)],
            dst_ref=buffer.at[band(source), :],
            send_sem=xkv_send.at[which, peer],
            recv_sem=xkv_recv.at[which, source],
            device_id=peer_id(peer),
            device_id_type=MESH,
        )

    def span_of(chunk):
        return pl.ds(pl.multiple_of(lax.rem(chunk, halves) * tile, tile), tile)

    def pass_q(owner, chunk, direction):
        piece = qall.at[owner, span_of(chunk), columns(chunk // halves)]
        return pltpu.make_async_remote_copy(
            src_ref=piece,
            dst_ref=piece,
            send_sem=zq_send.at[direction, owner, chunk],
            recv_sem=zq_recv.at[owner, chunk],
            device_id={"seq": at_seq + 2 * direction - 1},
            device_id_type=MESH,
        )

    def pass_out(owner, head, direction):
        slot = owner + direction
        to = {"seq": at_seq + 2 * direction - 1}
        return (
            pltpu.make_async_remote_copy(
                src_ref=msg_out.at[owner, head], dst_ref=msg_in.at[slot, head],
                send_sem=m_send.at[owner, head], recv_sem=m_recv.at[slot, head],
                device_id=to, device_id_type=MESH,
            ),
            pltpu.make_async_remote_copy(
                src_ref=st_out.at[owner, head], dst_ref=st_in.at[slot, head],
                send_sem=t_send.at[owner, head], recv_sem=t_recv.at[slot, head],
                device_id=to, device_id_type=MESH,
            ),
        )

    def got_out(slot, head):
        to = {"seq": lax.rem(at_seq + 1, seq_count)}
        return (
            pltpu.make_async_remote_copy(
                src_ref=msg_out.at[0, head], dst_ref=msg_in.at[slot, head],
                send_sem=m_send.at[0, head], recv_sem=m_recv.at[slot, head],
                device_id=to, device_id_type=MESH,
            ),
            pltpu.make_async_remote_copy(
                src_ref=st_out.at[0, head], dst_ref=st_in.at[slot, head],
                send_sem=t_send.at[0, head], recv_sem=t_recv.at[slot, head],
                device_id=to, device_id_type=MESH,
            ),
        )

    def spread_out(peer, source, head):
        return pltpu.make_async_remote_copy(
            src_ref=fin.at[band(peer), columns(head)],
            dst_ref=out_ref.at[:, head_cols(source, head)],
            send_sem=o_send.at[head, peer],
            recv_sem=o_recv.at[head, source],
            device_id=peer_id(peer),
            device_id_type=MESH,
        )

    def keep_out(head):
        return pltpu.make_async_copy(
            fin.at[band(place), columns(head)],
            out_ref.at[:, head_cols(place, head)],
            o_loc.at[head],
        )

    def each_head(fn):
        pl.loop(0, head_count)(fn)

    @functools.partial(each_head)
    def _(head):
        for step in range(1, peers):
            spread_q(peer_of(step), head).start()

    for which in range(2):
        for step in range(1, peers):
            spread_kv(which, peer_of(step), place).start()

    def own_ready(chunk):
        for index in range(bands):
            peer = lax.rem(chunk, halves) * bands + index

            @pl.when(peer != place)
            def _(peer=peer):
                landed_q(peer, chunk // halves).wait_recv()

    own[0].wait()
    own_ready(0)
    for direction, there in ((0, has_left), (1, has_right)):
        @pl.when(there)
        def _(direction=direction):
            pass_q(at_seq, 0, direction).start()

    own[4].wait()

    @functools.partial(each_head)
    def _(head):
        for block in range(cache_blocks):
            piece = vc[block * BLOCK:(block + 1) * BLOCK, columns(head)]
            vt[head, :, block * BLOCK:(block + 1) * BLOCK] = (
                piece.astype(jnp.float32).T.astype(jnp.bfloat16)
            )

    own[3].wait()

    def attend(keys, values_t, queries, causal):
        scores = lax.dot_general(
            keys, queries, (((1,), (1,)), ((), ())), preferred_element_type=jnp.float32
        )
        if causal is not None:
            scores = jnp.where(causal, scores, -jnp.inf)
        top = jnp.max(scores, axis=0, keepdims=True)
        weights = jnp.exp2((scores - top) * scaling)
        total = jnp.sum(weights, axis=0, keepdims=True)
        mixed = jnp.dot(
            values_t, weights.astype(jnp.bfloat16), preferred_element_type=jnp.float32
        )
        return mixed, top * scaling, total

    def join(a, b):
        top = jnp.maximum(a[1], b[1])
        fa, fb = jnp.exp2(a[1] - top), jnp.exp2(b[1] - top)
        return a[0] * fa + b[0] * fb, top, a[2] * fa + b[2] * fb

    def put_part(owner, chunk, result):
        part[owner, chunk] = result[0]
        pst[owner, chunk, 0:1] = result[1]
        pst[owner, chunk, 1:2] = result[2]

    def get_part(owner, chunk):
        return part[owner, chunk], pst[owner, chunk, 0:1], pst[owner, chunk, 1:2]

    def cached_part(owner, chunk):
        head = chunk // halves
        queries = qall[owner, span_of(chunk), columns(head)]
        result = None
        for block in range(cache_blocks):
            piece = attend(
                kc[block * BLOCK:(block + 1) * BLOCK, columns(head)],
                vt[head, :, block * BLOCK:(block + 1) * BLOCK],
                queries,
                None,
            )
            result = piece if result is None else join(result, piece)
        put_part(owner, chunk, result)

    def own_part(chunk):
        head = chunk // halves
        queries = qall[at_seq, span_of(chunk), columns(head)]
        for at in range(halves):
            @pl.when(lax.rem(chunk, halves) == at)
            def _(at=at):
                depth = (at + 1) * tile
                key_at = lax.broadcasted_iota(jnp.int32, (depth, tile), 0)
                query_at = lax.broadcasted_iota(jnp.int32, (depth, tile), 1) + at * tile
                values_t = vown[0:depth, columns(head)].astype(jnp.float32).T
                piece = attend(
                    kown[0:depth, columns(head)],
                    values_t.astype(jnp.bfloat16),
                    queries,
                    key_at <= query_at,
                )
                put_part(at_seq, chunk, join(piece, get_part(at_seq, chunk)))

    lanes = min(tile, 128)
    folds = tile // lanes

    def fold_stats(owner, chunk, which, row):
        for index in range(folds):
            st_out[owner, chunk, which * folds + index:which * folds + index + 1] = row[
                :, index * lanes:(index + 1) * lanes
            ]

    def unfold_stats(slot, chunk, which):
        rows_of = [
            st_in[slot, chunk, which * folds + index:which * folds + index + 1]
            for index in range(folds)
        ]
        return jnp.concatenate(rows_of, axis=1)

    def take_in(slot, owner, chunk):
        for copy in got_out(slot, chunk):
            copy.wait_recv()
        mixed = msg_in[slot, chunk].astype(jnp.float32) * unfold_stats(slot, chunk, 1)
        level = unfold_stats(slot, chunk, 0)
        other = (mixed, level, jnp.ones_like(level))
        put_part(owner, chunk, join(get_part(owner, chunk), other))

    def inside(index, limit):
        return jnp.logical_and(index >= 0, index < limit)

    def foreign(index):
        distance = index // 2 + 1
        direction = lax.rem(index, 2)
        return at_seq + (2 * direction - 1) * distance, direction, distance

    def fold(owner, chunk):
        right = (owner > at_seq).astype(jnp.int32)

        @pl.when(inside(at_seq - 2 * right + 1, seq_count))
        def _():
            take_in(owner + right, owner, chunk)

        mixed = part[owner, chunk]
        total = pst[owner, chunk, 1:2]
        most = jnp.maximum(jnp.max(jnp.abs(mixed), axis=0, keepdims=True), 1e-30)
        msg_out[owner, chunk] = (
            jnp.round(mixed * (32767.0 / most)).astype(jnp.int32).astype(jnp.int16)
        )
        fold_stats(owner, chunk, 0, pst[owner, chunk, 0:1] + jnp.log2(total))
        fold_stats(owner, chunk, 1, most * (1.0 / 32767.0) / total)

    def load():
        own[1].wait()
        own[2].wait()
        for which in range(2):
            for step in range(1, peers):
                peer = peer_of(step)
                spread_kv(which, peer, peer).wait_recv()

    def close(chunk):
        head = chunk // halves
        for side, there in ((1, has_left), (0, has_right)):
            @pl.when(there)
            def _(side=side):
                take_in(at_seq + side, at_seq, chunk)

        done = part[at_seq, chunk] / pst[at_seq, chunk, 1:2]
        fin[span_of(chunk), columns(head)] = done.T.astype(jnp.bfloat16)
        for index in range(bands):
            peer = lax.rem(chunk, halves) * bands + index

            @pl.when(peer != place)
            def _(peer=peer):
                spread_out(peer, place, head).start()

            @pl.when(peer == place)
            def _():
                keep_out(head).start()

    def emit(owner, chunk):
        for copy in pass_out(owner, chunk, (owner > at_seq).astype(jnp.int32)):
            copy.start()

    def step(code):
        kind, rest = lax.rem(code, KINDS), code // KINDS
        direction, rest = lax.rem(rest, 2), rest // 2
        owner, chunk = lax.rem(rest, seq_count), rest // seq_count

        @pl.when(kind <= TAKE)
        def _():
            @pl.when(kind == READY)
            def _():
                own_ready(chunk)

            @pl.when(kind == TAKE)
            def _():
                pass_q(owner, chunk, 0).wait_recv()

            @pl.when(kind == PASS)
            def _():
                pass_q(owner, chunk, direction).start()

        @pl.when(jnp.logical_and(kind > TAKE, kind <= OWN))
        def _():
            @pl.when(kind == WORK)
            def _():
                cached_part(owner, chunk)

            @pl.when(kind == LOAD)
            def _():
                load()

            @pl.when(kind == OWN)
            def _():
                own_part(chunk)

        @pl.when(kind > OWN)
        def _():
            @pl.when(kind == FOLD)
            def _():
                fold(owner, chunk)

            @pl.when(kind == EMIT)
            def _():
                emit(owner, chunk)

            @pl.when(kind == DONE)
            def _():
                close(chunk)

    @pl.loop(0, len(words))
    def _(index):
        word = pick_word(words, index)

        @pl.loop(0, each)
        def _(field):
            code = lax.rem(word, base)
            for k in range(1, each):
                code = jnp.where(field == k, lax.rem(lax.div(word, base**k), base), code)
            step(code)

    @functools.partial(each_head)
    def _(head):
        for step in range(1, peers):
            peer = peer_of(step)
            spread_out(peer, peer, head).wait_recv()
            spread_out(peer, place, head).wait_send()
            spread_q(peer, head).wait_send()
        keep_out(head).wait()

    @pl.loop(0, chunks)
    def _(chunk):
        for direction, there in ((0, has_left), (1, has_right)):
            @pl.when(there)
            def _(direction=direction):
                pass_q(at_seq, chunk, direction).wait_send()

        @pl.loop(0, 2 * (seq_count - 1))
        def _(index):
            owner, direction, distance = foreign(index)

            @pl.when(inside(owner, seq_count))
            def _():
                for copy in pass_out(owner, chunk, direction):
                    copy.wait_send()
                onward = 1 - direction

                @pl.when(inside(at_seq + 2 * onward - 1, seq_count))
                def _():
                    pass_q(owner, chunk, onward).wait_send()

    for which in range(2):
        for step in range(1, peers):
            spread_kv(which, peer_of(step), place).wait_send()


def dense_body(queries, new_keys, new_values, cache_keys, cache_values):
    seq_count = lax.axis_size("seq")
    heads_size, sub_size = lax.axis_size("heads"), lax.axis_size("sub")
    peers = heads_size * sub_size
    rows, width = queries.shape
    cached, span_cols = cache_keys.shape
    head_count, length = span_cols // HD, rows * peers
    tile = span_tile(rows, length)
    chunks = head_count * (length // tile)
    lanes = min(tile, 128)
    stat_rows = 2 * (tile // lanes)
    dma = pltpu.SemaphoreType.DMA
    anywhere = pl.BlockSpec(memory_space=pltpu.HBM)
    return pl.pallas_call(
        functools.partial(fused_kernel, seq_count, heads_size, sub_size, head_count),
        out_shape=jax.ShapeDtypeStruct((rows, width), jnp.bfloat16),
        in_specs=[anywhere] * 5,
        out_specs=pl.BlockSpec(memory_space=pltpu.VMEM),
        scratch_shapes=[
            pltpu.VMEM((seq_count, length, span_cols), jnp.bfloat16),
            pltpu.VMEM((length, span_cols), jnp.bfloat16),
            pltpu.VMEM((length, span_cols), jnp.bfloat16),
            pltpu.VMEM((cached, span_cols), jnp.bfloat16),
            pltpu.VMEM((cached, span_cols), jnp.bfloat16),
            pltpu.VMEM((head_count, HD, cached), jnp.bfloat16),
            pltpu.VMEM((seq_count + 1, chunks, HD, tile), jnp.int16),
            pltpu.VMEM((seq_count + 1, chunks, stat_rows, lanes), jnp.float32),
            pltpu.VMEM((seq_count, chunks, HD, tile), jnp.int16),
            pltpu.VMEM((seq_count, chunks, stat_rows, lanes), jnp.float32),
            pltpu.VMEM((seq_count, chunks, HD, tile), jnp.float32),
            pltpu.VMEM((seq_count, chunks, 8, tile), jnp.float32),
            pltpu.VMEM((length, span_cols), jnp.bfloat16),
            dma((5,)),
            dma((head_count, peers)),
            dma((head_count, peers)),
            dma((2, peers)),
            dma((2, peers)),
            dma((2, seq_count, chunks)),
            dma((seq_count, chunks)),
            dma((seq_count, chunks)),
            dma((seq_count + 1, chunks)),
            dma((seq_count, chunks)),
            dma((seq_count + 1, chunks)),
            dma((head_count, peers)),
            dma((head_count, peers)),
            dma((head_count,)),
        ],
        compiler_params=pltpu.CompilerParams(
            collective_id=0, has_side_effects=True, vmem_limit_bytes=60 * 1024 * 1024
        ),
    )(queries, new_keys, new_values, cache_keys, cache_values)


def order_ranks(owners):
    length = owners.shape[-1]
    counter = jnp.arange(length)
    earlier = counter[None, :] < counter[:, None]
    same_owner = owners[..., :, None] == owners[..., None, :]
    return jnp.sum(jnp.logical_and(same_owner, earlier), axis=-1)


def one_hot(values, length):
    return (values[..., None] == jnp.arange(length)).astype(jnp.float32)


def own_partial(query_blocks, key_blocks, value_blocks, scaling):
    scores = (
        jnp.einsum("bqhd,bkhd->bhqk", query_blocks, key_blocks, preferred_element_type=jnp.float32)
        * scaling
    )
    length = query_blocks.shape[1]
    causal = jnp.arange(length)[:, None] >= jnp.arange(length)[None, :]
    scores = jnp.where(causal, scores, -jnp.inf)
    highest = jnp.max(scores, axis=-1)
    weights = jnp.exp(scores - highest[..., None])
    totals = jnp.sum(weights, axis=-1)
    mixed = jnp.einsum(
        "bhqk,bkhd->bhqd",
        weights.astype(jnp.bfloat16),
        value_blocks,
        preferred_element_type=jnp.float32,
    )
    return (mixed, highest, totals)


def tile_partial(query_blocks, tile_pair, scaling):
    head_size = query_blocks.shape[-1]
    scores = (
        jnp.einsum(
            "bqhd,bhkd->bhqk",
            query_blocks,
            tile_pair[..., :head_size],
            preferred_element_type=jnp.float32,
        )
        * scaling
    )
    highest = jnp.max(scores, axis=-1)
    weights = jnp.exp(scores - highest[..., None])
    totals = jnp.sum(weights, axis=-1)
    mixed = jnp.einsum(
        "bhqk,bhkd->bhqd",
        weights.astype(jnp.bfloat16),
        tile_pair[..., head_size:],
        preferred_element_type=jnp.float32,
    )
    return (mixed, highest, totals)


def merge_parts(parts):
    top = parts[0][1]
    for part in parts[1:]:
        top = jnp.maximum(top, part[1])
    numer = jnp.zeros(parts[0][0].shape, jnp.float32)
    denom = jnp.zeros(parts[0][2].shape, jnp.float32)
    for part in parts:
        factor = jnp.exp(part[1] - top)
        numer = numer + factor[..., None] * part[0]
        denom = denom + factor * part[2]
    return numer / denom[..., None]


def general_body(queries, new_keys, new_values, cache_keys, cache_values, selection):
    heads_q, heads_k, heads_v = (
        lax.all_to_all(queries, ("heads", "sub"), split_axis=1, concat_axis=0, tiled=True),
        lax.all_to_all(new_keys, ("heads", "sub"), split_axis=1, concat_axis=0, tiled=True),
        lax.all_to_all(new_values, ("heads", "sub"), split_axis=1, concat_axis=0, tiled=True),
    )
    qblocks, head_count, top_count = selection.shape
    head_size = HD
    scaling = head_size ** (-0.5)
    shaped = (qblocks, BLOCK, head_count, head_size)
    query_blocks = heads_q.reshape(shaped)
    own = own_partial(query_blocks, heads_k.reshape(shaped), heads_v.reshape(shaped), scaling)
    seq_count = lax.axis_size("seq")
    myself = lax.axis_index("seq")
    cache_blocks = cache_keys.shape[0] // BLOCK
    tile_count = cache_blocks * head_count
    request_count = qblocks * head_count * top_count
    capacity = -(-request_count // seq_count)
    requests_all = lax.all_gather(selection, "seq", axis=0, tiled=True).reshape(
        seq_count, request_count
    )
    head_of = jnp.arange(request_count) // top_count % head_count
    my_requests = selection.reshape(request_count)
    my_owner = my_requests // cache_blocks
    my_slot = my_owner * capacity + order_ranks(my_owner)
    key_tiles = cache_keys.reshape(cache_blocks, BLOCK, head_count, head_size).transpose(0, 2, 1, 3)
    value_tiles = cache_values.reshape(cache_blocks, BLOCK, head_count, head_size).transpose(
        0, 2, 1, 3
    )
    tile_set = jnp.concatenate([key_tiles, value_tiles], axis=-1).reshape(
        tile_count, BLOCK, 2 * head_size
    )
    their_owner = requests_all // cache_blocks
    local_tile = requests_all % cache_blocks * head_count + head_of[None, :]
    served = (their_owner == myself).astype(jnp.float32)
    slot_pick = one_hot(order_ranks(their_owner), capacity) * served[..., None]
    picking = jnp.einsum("erc,erl->ecl", slot_pick, one_hot(local_tile, tile_count)).astype(
        jnp.bfloat16
    )
    parts = [own]
    outgoing = jnp.einsum(
        "ecl,lkf->eckf", picking, tile_set, preferred_element_type=jnp.float32
    ).astype(jnp.bfloat16)
    incoming = lax.all_to_all(outgoing, "seq", split_axis=0, concat_axis=0, tiled=True)
    fetched = incoming.reshape(seq_count * capacity, BLOCK, 2 * head_size)[my_slot]
    fetched = fetched.reshape(qblocks, head_count, top_count, BLOCK, 2 * head_size)
    for turn in range(top_count):
        parts.append(tile_partial(query_blocks, fetched[:, :, turn], scaling))
    result = merge_parts(parts)
    result = (
        result.transpose(0, 2, 1, 3)
        .reshape(qblocks * BLOCK, head_count * head_size)
        .astype(jnp.bfloat16)
    )
    return lax.all_to_all(result, ("heads", "sub"), split_axis=0, concat_axis=1, tiled=True)


def body(queries, new_keys, new_values, cache_keys, cache_values, selection):
    qblocks, head_count, top_count = selection.shape
    blocks_total = cache_keys.shape[0] // BLOCK * lax.axis_size("seq")
    if blocks_total == top_count and qblocks == 1:
        return dense_body(queries, new_keys, new_values, cache_keys, cache_values)
    return general_body(queries, new_keys, new_values, cache_keys, cache_values, selection)


def solution(mesh):
    in_specs = (
        P(("groups", "seq", "heads", "sub"), None),
        P(("groups", "seq", "heads", "sub"), None),
        P(("groups", "seq", "heads", "sub"), None),
        P(("groups", "seq"), ("heads", "sub")),
        P(("groups", "seq"), ("heads", "sub")),
        P(("groups", "seq"), ("heads", "sub"), None),
    )
    out_specs = P(("groups", "seq", "heads", "sub"), None)
    return jax.shard_map(body, mesh=mesh, in_specs=in_specs, out_specs=out_specs, check_vma=False)
```

```python
import functools
import heapq
import math

import jax
import jax.numpy as jnp
from jax import lax
from jax.experimental import pallas as pl
from jax.experimental.pallas import tpu as pltpu
from jax.sharding import PartitionSpec as P

HD = 128
BLOCK = 512


MESH = pl.DeviceIdType.MESH
TILE = 256
KEYS = 256

READY, TAKE, PASS, START, RELAY, WORK, OWN, LOAD, FOLD, EMIT, DONE, REST = range(12)
KINDS = 16
SEND, UNIT, SPAN, MERGE, CLOSE, WIRE, HOP = 0.08, 0.68, 0.35, 0.28, 0.4, 1.43, 2.0
FIRST, EACH, LATE, DEEP = 2.0, 0.7, 21.0, 3
K_FAR, K_OUT, K_DIST, K_OWN, W_DIST, W_SELF, W_OWN = 1.0, 8.0, 2.0, 3.0, 1.0, 0.0, 3.5


def plan_steps(count, chunks, group):
    steps = [[] for _ in range(count)]
    free = [0.0] * count
    seen, back = ([{} for _ in range(count)] for _ in range(2))
    touched, passed, worked, owned, folded, emitted, finished = (
        [set() for _ in range(count)] for _ in range(7)
    )
    wires = {(s, d): [] for s in range(count) for d in (-1, 1) if 0 <= s + d < count}
    heap = []
    for s in range(count):
        for n in range(chunks):
            seen[s][s, n] = FIRST + EACH * n
            heapq.heappush(heap, (seen[s][s, n], s))
        heapq.heappush(heap, (LATE, s))

    def first_use(s, o, n):
        if (o, n) not in touched[s]:
            touched[s].add((o, n))
            steps[s].append((READY if o == s else TAKE, o, n, 0))

    def launch(t, s, d, arrive, entry):
        finish = max([t] + wires[s, d][-1:]) + WIRE
        wires[s, d].append(finish)
        arrive[s + d][entry] = finish + HOP
        heapq.heappush(heap, (finish + HOP, s + d))
        heapq.heappush(heap, (finish, s))

    def next_send(t, s, d):
        found = []
        for (o, n), when in seen[s].items():
            onward = o == s or (o < s) == (d > 0)
            if when <= t and onward and (o, n, d) not in passed[s]:
                left = count - 1 - s if d > 0 else s
                found.append((n - K_FAR * left + (K_OWN if o == s else 0.0), 0, o, n))
        for o, n in folded[s]:
            if (o - s) * d > 0 and (o, n) not in emitted[s]:
                found.append((n + K_OUT - K_DIST * abs(o - s), 1, o, n))
        return min(found) if found else None

    def next_work(t, s):
        found = []
        for o, n in worked[s]:
            if o != s and (o, n) not in folded[s]:
                far = s + (s - o) // abs(s - o)
                if not 0 <= far < count or back[s].get((o, n), t + 1) <= t:
                    found.append((0, n - 2 * abs(o - s), FOLD, o, n, MERGE))
        for n in range(chunks):
            if (s, n) in worked[s] and n in owned[s] and n not in finished[s]:
                sides = [d for d in (-1, 1) if (s, d) in wires]
                if all(back[s].get((s, n, d), t + 1) <= t for d in sides):
                    found.append((1, n, DONE, s, n, CLOSE))
        for n in range(0, chunks, group):
            for o in range(count):
                here = all(seen[s].get((o, n + k), t + 1) <= t for k in range(group))
                if here and (o, n) not in worked[s]:
                    rank = n - (W_DIST * abs(o - s) if o != s else W_SELF)
                    found.append((2, rank, WORK, o, n, UNIT * group))
            if t >= LATE and n not in owned[s] and (s, n) in worked[s]:
                found.append((2, n + W_OWN, OWN, s, n, SPAN * group))
        return min(found) if found else None

    while heap:
        t, s = heapq.heappop(heap)
        if t < free[s] - 1e-9:
            continue
        for d in (-1, 1):
            while (s, d) in wires and sum(f > t for f in wires[s, d]) < DEEP:
                best = next_send(t, s, d)
                if best is None:
                    break
                _, out, o, n = best
                if out:
                    emitted[s].add((o, n))
                    steps[s].append((EMIT, o, n, d))
                    launch(t, s, d, back, (o, n, -d) if s + d == o else (o, n))
                else:
                    first_use(s, o, n)
                    passed[s].add((o, n, d))
                    steps[s].append((PASS, o, n, d))
                    launch(t, s, d, seen, (o, n))
                t += SEND
        best = next_work(t, s)
        free[s] = t
        if best is None:
            continue
        _, _, kind, o, n, price = best
        if kind == WORK:
            for k in range(group):
                first_use(s, o, n + k)
                worked[s].add((o, n + k))
        elif kind == OWN:
            if not owned[s]:
                steps[s].append((LOAD, o, n, 0))
            owned[s].update(range(n, n + group))
        elif kind == FOLD:
            folded[s].add((o, n))
        else:
            finished[s].add(n)
        steps[s].append((kind, o, n, 0))
        free[s] = t + price
        heapq.heappush(heap, (free[s], s))
    return steps


def join_steps(steps):
    joined = []
    for kind, o, n, d in steps:
        if kind == PASS and joined and joined[-1][1:3] == (o, n):
            if joined[-1][0] in (READY, TAKE):
                joined[-1] = (START if joined[-1][0] == READY else RELAY, o, n, d)
                continue
        joined.append((kind, o, n, d))
    return joined


def plan_codes(count, chunks, group):
    steps = plan_steps(count, chunks, group)
    codes = []
    for s, one in enumerate(steps):
        one = [x for x in one if not (x[1:3] == (s, 0) and x[0] in (READY, PASS))]
        row = [k + KINDS * ((d > 0) + 2 * (o + count * n)) for k, o, n, d in join_steps(one)]
        codes.append(row)
    base = KINDS * 2 * count * chunks
    each = max(k for k in range(1, 8) if base**k < 2**31)
    longest = -(-max(len(row) for row in codes) // each)
    words = []
    for row in codes:
        row = row + [REST] * (longest * each - len(row))
        words.append(
            [sum(row[w * each + k] * base**k for k in range(each)) for w in range(longest)]
        )
    return words, base, each


def pick_word(words, index):
    if len(words) == 1:
        return words[0]
    half = 1 << (len(words) - 1).bit_length() - 1
    low, high = words[:half], words[half:]
    return jnp.where(index >= half, pick_word(high, index - half), pick_word(low, index))


def span_tile(rows, length):
    return min(length, max(rows, TILE))


def columns(head):
    return pl.ds(pl.multiple_of(head * HD, HD), HD)


def fused_kernel(
    seq_count, heads_size, sub_size, head_count,
    q_ref, k_ref, v_ref, ck_ref, cv_ref, out_ref,
    qall, kown, vown, kc, vc, vt, msg_in, st_in, msg_out, st_out, part, pst, fin,
    loc_sem, xq_send, xq_recv, xkv_send, xkv_recv, zq_send, zq_recv,
    m_send, m_recv, t_send, t_recv, o_send, o_recv, o_loc,
):
    peers = heads_size * sub_size
    rows, span_cols = q_ref.shape[0], head_count * HD
    length = rows * peers
    tile = span_tile(rows, length)
    halves, bands = length // tile, tile // rows
    chunks = head_count * halves
    cache_blocks = kc.shape[0] // BLOCK
    scaling = HD ** (-0.5) * math.log2(math.e)
    at_seq = lax.axis_index("seq")
    place = lax.axis_index("heads") * sub_size + lax.axis_index("sub")
    has_left, has_right = at_seq > 0, at_seq < seq_count - 1

    def peer_of(step):
        return lax.rem(place + step, peers)

    def peer_id(peer):
        return {"heads": peer // sub_size, "sub": lax.rem(peer, sub_size)}

    def band(index):
        return pl.ds(pl.multiple_of(index * rows, rows), rows)

    def slab(index):
        return pl.ds(pl.multiple_of(index * span_cols, span_cols), span_cols)

    def head_cols(peer, head):
        return pl.ds(pl.multiple_of(peer * span_cols + head * HD, HD), HD)

    barrier = pltpu.get_barrier_semaphore()
    for step in range(1, peers):
        pl.semaphore_signal(barrier, inc=1, device_id=peer_id(peer_of(step)), device_id_type=MESH)

    @pl.when(has_left)
    def _():
        pl.semaphore_signal(barrier, inc=1, device_id={"seq": at_seq - 1}, device_id_type=MESH)

    @pl.when(has_right)
    def _():
        pl.semaphore_signal(barrier, inc=1, device_id={"seq": at_seq + 1}, device_id_type=MESH)

    own = [
        pltpu.make_async_copy(
            q_ref.at[:, slab(place)], qall.at[at_seq, band(place), :], loc_sem.at[0]
        ),
        pltpu.make_async_copy(k_ref.at[:, slab(place)], kown.at[band(place), :], loc_sem.at[1]),
        pltpu.make_async_copy(v_ref.at[:, slab(place)], vown.at[band(place), :], loc_sem.at[2]),
        pltpu.make_async_copy(ck_ref, kc, loc_sem.at[3]),
        pltpu.make_async_copy(cv_ref, vc, loc_sem.at[4]),
    ]
    for copy in (own[0], own[4], own[3], own[1], own[2]):
        copy.start()
    plans, base, each = plan_codes(seq_count, chunks, halves)
    words = []
    for index in range(len(plans[0])):
        value = jnp.int32(plans[0][index])
        for s in range(1, seq_count):
            value = jnp.where(at_seq == s, jnp.int32(plans[s][index]), value)
        words.append(value)
    sides = has_left.astype(jnp.int32) + has_right.astype(jnp.int32)
    pl.semaphore_wait(barrier, peers - 1 + sides)

    def spread_q(peer, head):
        return pltpu.make_async_remote_copy(
            src_ref=q_ref.at[:, head_cols(peer, head)],
            dst_ref=qall.at[at_seq, band(place), columns(head)],
            send_sem=xq_send.at[head, peer],
            recv_sem=xq_recv.at[head, place],
            device_id=peer_id(peer),
            device_id_type=MESH,
        )

    def landed_q(peer, head):
        return pltpu.make_async_remote_copy(
            src_ref=q_ref.at[:, head_cols(peer, head)],
            dst_ref=qall.at[at_seq, band(peer), columns(head)],
            send_sem=xq_send.at[head, peer],
            recv_sem=xq_recv.at[head, peer],
            device_id=peer_id(peer),
            device_id_type=MESH,
        )

    def spread_kv(which, peer, source):
        ref, buffer = ((k_ref, kown), (v_ref, vown))[which]
        return pltpu.make_async_remote_copy(
            src_ref=ref.at[:, slab(peer)],
            dst_ref=buffer.at[band(source), :],
            send_sem=xkv_send.at[which, peer],
            recv_sem=xkv_recv.at[which, source],
            device_id=peer_id(peer),
            device_id_type=MESH,
        )

    def span_of(chunk):
        return pl.ds(pl.multiple_of(lax.rem(chunk, halves) * tile, tile), tile)

    def pass_q(owner, chunk, direction):
        piece = qall.at[owner, span_of(chunk), columns(lax.div(chunk, halves))]
        return pltpu.make_async_remote_copy(
            src_ref=piece,
            dst_ref=piece,
            send_sem=zq_send.at[direction, owner, chunk],
            recv_sem=zq_recv.at[owner, chunk],
            device_id={"seq": at_seq + 2 * direction - 1},
            device_id_type=MESH,
        )

    def pass_out(owner, head, direction):
        slot = owner + direction
        to = {"seq": at_seq + 2 * direction - 1}
        return (
            pltpu.make_async_remote_copy(
                src_ref=msg_out.at[owner, head], dst_ref=msg_in.at[slot, head],
                send_sem=m_send.at[owner, head], recv_sem=m_recv.at[slot, head],
                device_id=to, device_id_type=MESH,
            ),
            pltpu.make_async_remote_copy(
                src_ref=st_out.at[owner, head], dst_ref=st_in.at[slot, head],
                send_sem=t_send.at[owner, head], recv_sem=t_recv.at[slot, head],
                device_id=to, device_id_type=MESH,
            ),
        )

    def got_out(slot, head):
        to = {"seq": lax.rem(at_seq + 1, seq_count)}
        return (
            pltpu.make_async_remote_copy(
                src_ref=msg_out.at[0, head], dst_ref=msg_in.at[slot, head],
                send_sem=m_send.at[0, head], recv_sem=m_recv.at[slot, head],
                device_id=to, device_id_type=MESH,
            ),
            pltpu.make_async_remote_copy(
                src_ref=st_out.at[0, head], dst_ref=st_in.at[slot, head],
                send_sem=t_send.at[0, head], recv_sem=t_recv.at[slot, head],
                device_id=to, device_id_type=MESH,
            ),
        )

    def spread_out(peer, source, head):
        return pltpu.make_async_remote_copy(
            src_ref=fin.at[band(peer), columns(head)],
            dst_ref=out_ref.at[:, head_cols(source, head)],
            send_sem=o_send.at[head, peer],
            recv_sem=o_recv.at[head, source],
            device_id=peer_id(peer),
            device_id_type=MESH,
        )

    def keep_out(head):
        return pltpu.make_async_copy(
            fin.at[band(place), columns(head)],
            out_ref.at[:, head_cols(place, head)],
            o_loc.at[head],
        )

    def each_head(fn):
        pl.loop(0, head_count)(fn)

    @functools.partial(each_head)
    def _(head):
        for step in range(1, peers):
            spread_q(peer_of(step), head).start()

    for which in range(2):
        for step in range(1, peers):
            spread_kv(which, peer_of(step), place).start()

    def own_ready(chunk):
        for index in range(bands):
            peer = lax.rem(chunk, halves) * bands + index

            @pl.when(peer != place)
            def _(peer=peer):
                landed_q(peer, lax.div(chunk, halves)).wait_recv()

    own[0].wait()
    own_ready(0)
    for direction, there in ((0, has_left), (1, has_right)):
        @pl.when(there)
        def _(direction=direction):
            pass_q(at_seq, 0, direction).start()

    own[4].wait()

    @functools.partial(each_head)
    def _(head):
        for block in range(cache_blocks):
            piece = vc[block * BLOCK:(block + 1) * BLOCK, columns(head)]
            vt[head, :, block * BLOCK:(block + 1) * BLOCK] = (
                piece.astype(jnp.float32).T.astype(jnp.bfloat16)
            )

    own[3].wait()

    def attend(keys, values_t, queries, causal=None):
        count = keys.shape[0] // KEYS
        scores = []
        for at in range(count):
            score = lax.dot_general(
                keys[at * KEYS:(at + 1) * KEYS],
                queries,
                (((1,), (1,)), ((), ())),
                preferred_element_type=jnp.float32,
            )
            if causal is not None:
                score = jnp.where(causal[at * KEYS:(at + 1) * KEYS], score, -jnp.inf)
            scores.append(score)
        tops = [jnp.max(score, axis=0, keepdims=True) for score in scores]
        top = functools.reduce(jnp.maximum, tops) * scaling
        mixed = total = 0.0
        for at, score in enumerate(scores):
            weights = jnp.exp2(score * scaling - top)
            total = total + jnp.sum(weights, axis=0, keepdims=True)
            mixed = mixed + jnp.dot(
                values_t[:, at * KEYS:(at + 1) * KEYS],
                weights.astype(jnp.bfloat16),
                preferred_element_type=jnp.float32,
            )
        return mixed, top, total

    def join(a, b):
        top = jnp.maximum(a[1], b[1])
        fa, fb = jnp.exp2(a[1] - top), jnp.exp2(b[1] - top)
        return a[0] * fa + b[0] * fb, top, a[2] * fa + b[2] * fb

    def put_part(owner, chunk, result):
        part[owner, chunk] = result[0]
        pst[owner, chunk, 0:1] = result[1]
        pst[owner, chunk, 1:2] = result[2]

    def get_part(owner, chunk):
        return part[owner, chunk], pst[owner, chunk, 0:1], pst[owner, chunk, 1:2]

    def cached_part(owner, chunk):
        head = lax.div(chunk, halves)
        keys, values_t = kc[:, columns(head)], vt[head]
        for at in range(halves):
            queries = qall[owner, at * tile:(at + 1) * tile, columns(head)]
            put_part(owner, chunk + at, attend(keys, values_t, queries))

    def own_part(chunk):
        head = lax.div(chunk, halves)
        keys = kown[:, columns(head)]
        values_t = vown[:, columns(head)].astype(jnp.float32).T.astype(jnp.bfloat16)
        for at in range(halves):
            depth = (at + 1) * tile
            key_at = lax.broadcasted_iota(jnp.int32, (depth, tile), 0)
            query_at = lax.broadcasted_iota(jnp.int32, (depth, tile), 1) + at * tile
            queries = qall[at_seq, at * tile:(at + 1) * tile, columns(head)]
            piece = attend(keys[0:depth], values_t[:, 0:depth], queries, key_at <= query_at)
            put_part(at_seq, chunk + at, join(piece, get_part(at_seq, chunk + at)))

    lanes = min(tile, 128)
    folds = tile // lanes

    def fold_stats(owner, chunk, which, row):
        for index in range(folds):
            st_out[owner, chunk, which * folds + index:which * folds + index + 1] = row[
                :, index * lanes:(index + 1) * lanes
            ]

    def unfold_stats(slot, chunk, which):
        rows_of = [
            st_in[slot, chunk, which * folds + index:which * folds + index + 1]
            for index in range(folds)
        ]
        return jnp.concatenate(rows_of, axis=1)

    def take_in(slot, owner, chunk):
        for copy in got_out(slot, chunk):
            copy.wait_recv()
        mixed = msg_in[slot, chunk].astype(jnp.float32) * unfold_stats(slot, chunk, 1)
        level = unfold_stats(slot, chunk, 0)
        other = (mixed, level, jnp.ones_like(level))
        put_part(owner, chunk, join(get_part(owner, chunk), other))

    def inside(index, limit):
        return jnp.logical_and(index >= 0, index < limit)

    def foreign(index):
        distance = index // 2 + 1
        direction = lax.rem(index, 2)
        return at_seq + (2 * direction - 1) * distance, direction, distance

    def fold(owner, chunk):
        right = (owner > at_seq).astype(jnp.int32)

        @pl.when(inside(at_seq - 2 * right + 1, seq_count))
        def _():
            take_in(owner + right, owner, chunk)

        mixed = part[owner, chunk]
        total = pst[owner, chunk, 1:2]
        most = jnp.maximum(jnp.max(jnp.abs(mixed), axis=0, keepdims=True), 1e-30)
        msg_out[owner, chunk] = (
            jnp.round(mixed * (32767.0 / most)).astype(jnp.int32).astype(jnp.int16)
        )
        fold_stats(owner, chunk, 0, pst[owner, chunk, 0:1] + jnp.log2(total))
        fold_stats(owner, chunk, 1, most * (1.0 / 32767.0) / total)

    def load():
        own[1].wait()
        own[2].wait()
        for which in range(2):
            for step in range(1, peers):
                peer = peer_of(step)
                spread_kv(which, peer, peer).wait_recv()

    def close(chunk):
        head = lax.div(chunk, halves)
        for side, there in ((1, has_left), (0, has_right)):
            @pl.when(there)
            def _(side=side):
                take_in(at_seq + side, at_seq, chunk)

        done = part[at_seq, chunk] / pst[at_seq, chunk, 1:2]
        fin[span_of(chunk), columns(head)] = done.T.astype(jnp.bfloat16)
        for index in range(bands):
            peer = lax.rem(chunk, halves) * bands + index

            @pl.when(peer != place)
            def _(peer=peer):
                spread_out(peer, place, head).start()

            @pl.when(peer == place)
            def _():
                keep_out(head).start()

    def emit(owner, chunk):
        for copy in pass_out(owner, chunk, (owner > at_seq).astype(jnp.int32)):
            copy.start()

    def step(code):
        kind, rest = lax.rem(code, KINDS), lax.div(code, KINDS)
        direction, rest = lax.rem(rest, 2), lax.div(rest, 2)
        owner, chunk = lax.rem(rest, seq_count), lax.div(rest, seq_count)

        @pl.when(kind <= RELAY)
        def _():
            @pl.when(jnp.logical_or(kind == READY, kind == START))
            def _():
                own_ready(chunk)

            @pl.when(jnp.logical_or(kind == TAKE, kind == RELAY))
            def _():
                pass_q(owner, chunk, 0).wait_recv()

            @pl.when(kind >= PASS)
            def _():
                pass_q(owner, chunk, direction).start()

        @pl.when(jnp.logical_and(kind > RELAY, kind < FOLD))
        def _():
            @pl.when(kind == WORK)
            def _():
                cached_part(owner, chunk)

            @pl.when(kind == OWN)
            def _():
                own_part(chunk)

            @pl.when(kind == LOAD)
            def _():
                load()

        @pl.when(kind >= FOLD)
        def _():
            @pl.when(kind == FOLD)
            def _():
                fold(owner, chunk)

            @pl.when(kind == EMIT)
            def _():
                emit(owner, chunk)

            @pl.when(kind == DONE)
            def _():
                close(chunk)

    @pl.loop(0, len(words))
    def _(index):
        word = pick_word(words, index)

        @pl.loop(0, each)
        def _(field):
            code = lax.rem(word, base)
            for k in range(1, each):
                code = jnp.where(field == k, lax.rem(lax.div(word, base**k), base), code)
            step(code)

    @functools.partial(each_head)
    def _(head):
        for step in range(1, peers):
            peer = peer_of(step)
            spread_out(peer, peer, head).wait_recv()
            spread_out(peer, place, head).wait_send()
            spread_q(peer, head).wait_send()
        keep_out(head).wait()

    @pl.loop(0, chunks)
    def _(chunk):
        for direction, there in ((0, has_left), (1, has_right)):
            @pl.when(there)
            def _(direction=direction):
                pass_q(at_seq, chunk, direction).wait_send()

        @pl.loop(0, 2 * (seq_count - 1))
        def _(index):
            owner, direction, distance = foreign(index)

            @pl.when(inside(owner, seq_count))
            def _():
                for copy in pass_out(owner, chunk, direction):
                    copy.wait_send()
                onward = 1 - direction

                @pl.when(inside(at_seq + 2 * onward - 1, seq_count))
                def _():
                    pass_q(owner, chunk, onward).wait_send()

    for which in range(2):
        for step in range(1, peers):
            spread_kv(which, peer_of(step), place).wait_send()


def dense_body(queries, new_keys, new_values, cache_keys, cache_values):
    seq_count = lax.axis_size("seq")
    heads_size, sub_size = lax.axis_size("heads"), lax.axis_size("sub")
    peers = heads_size * sub_size
    rows, width = queries.shape
    cached, span_cols = cache_keys.shape
    head_count, length = span_cols // HD, rows * peers
    tile = span_tile(rows, length)
    chunks = head_count * (length // tile)
    lanes = min(tile, 128)
    stat_rows = 2 * (tile // lanes)
    dma = pltpu.SemaphoreType.DMA
    anywhere = pl.BlockSpec(memory_space=pltpu.HBM)
    return pl.pallas_call(
        functools.partial(fused_kernel, seq_count, heads_size, sub_size, head_count),
        out_shape=jax.ShapeDtypeStruct((rows, width), jnp.bfloat16),
        in_specs=[anywhere] * 5,
        out_specs=pl.BlockSpec(memory_space=pltpu.VMEM),
        scratch_shapes=[
            pltpu.VMEM((seq_count, length, span_cols), jnp.bfloat16),
            pltpu.VMEM((length, span_cols), jnp.bfloat16),
            pltpu.VMEM((length, span_cols), jnp.bfloat16),
            pltpu.VMEM((cached, span_cols), jnp.bfloat16),
            pltpu.VMEM((cached, span_cols), jnp.bfloat16),
            pltpu.VMEM((head_count, HD, cached), jnp.bfloat16),
            pltpu.VMEM((seq_count + 1, chunks, HD, tile), jnp.int16),
            pltpu.VMEM((seq_count + 1, chunks, stat_rows, lanes), jnp.float32),
            pltpu.VMEM((seq_count, chunks, HD, tile), jnp.int16),
            pltpu.VMEM((seq_count, chunks, stat_rows, lanes), jnp.float32),
            pltpu.VMEM((seq_count, chunks, HD, tile), jnp.float32),
            pltpu.VMEM((seq_count, chunks, 8, tile), jnp.float32),
            pltpu.VMEM((length, span_cols), jnp.bfloat16),
            dma((5,)),
            dma((head_count, peers)),
            dma((head_count, peers)),
            dma((2, peers)),
            dma((2, peers)),
            dma((2, seq_count, chunks)),
            dma((seq_count, chunks)),
            dma((seq_count, chunks)),
            dma((seq_count + 1, chunks)),
            dma((seq_count, chunks)),
            dma((seq_count + 1, chunks)),
            dma((head_count, peers)),
            dma((head_count, peers)),
            dma((head_count,)),
        ],
        compiler_params=pltpu.CompilerParams(
            collective_id=0, has_side_effects=True, vmem_limit_bytes=60 * 1024 * 1024
        ),
    )(queries, new_keys, new_values, cache_keys, cache_values)


def order_ranks(owners):
    length = owners.shape[-1]
    counter = jnp.arange(length)
    earlier = counter[None, :] < counter[:, None]
    same_owner = owners[..., :, None] == owners[..., None, :]
    return jnp.sum(jnp.logical_and(same_owner, earlier), axis=-1)


def one_hot(values, length):
    return (values[..., None] == jnp.arange(length)).astype(jnp.float32)


def own_partial(query_blocks, key_blocks, value_blocks, scaling):
    scores = (
        jnp.einsum("bqhd,bkhd->bhqk", query_blocks, key_blocks, preferred_element_type=jnp.float32)
        * scaling
    )
    length = query_blocks.shape[1]
    causal = jnp.arange(length)[:, None] >= jnp.arange(length)[None, :]
    scores = jnp.where(causal, scores, -jnp.inf)
    highest = jnp.max(scores, axis=-1)
    weights = jnp.exp(scores - highest[..., None])
    totals = jnp.sum(weights, axis=-1)
    mixed = jnp.einsum(
        "bhqk,bkhd->bhqd",
        weights.astype(jnp.bfloat16),
        value_blocks,
        preferred_element_type=jnp.float32,
    )
    return (mixed, highest, totals)


def tile_partial(query_blocks, tile_pair, scaling):
    head_size = query_blocks.shape[-1]
    scores = (
        jnp.einsum(
            "bqhd,bhkd->bhqk",
            query_blocks,
            tile_pair[..., :head_size],
            preferred_element_type=jnp.float32,
        )
        * scaling
    )
    highest = jnp.max(scores, axis=-1)
    weights = jnp.exp(scores - highest[..., None])
    totals = jnp.sum(weights, axis=-1)
    mixed = jnp.einsum(
        "bhqk,bhkd->bhqd",
        weights.astype(jnp.bfloat16),
        tile_pair[..., head_size:],
        preferred_element_type=jnp.float32,
    )
    return (mixed, highest, totals)


def merge_parts(parts):
    top = parts[0][1]
    for part in parts[1:]:
        top = jnp.maximum(top, part[1])
    numer = jnp.zeros(parts[0][0].shape, jnp.float32)
    denom = jnp.zeros(parts[0][2].shape, jnp.float32)
    for part in parts:
        factor = jnp.exp(part[1] - top)
        numer = numer + factor[..., None] * part[0]
        denom = denom + factor * part[2]
    return numer / denom[..., None]


def general_body(queries, new_keys, new_values, cache_keys, cache_values, selection):
    heads_q, heads_k, heads_v = (
        lax.all_to_all(queries, ("heads", "sub"), split_axis=1, concat_axis=0, tiled=True),
        lax.all_to_all(new_keys, ("heads", "sub"), split_axis=1, concat_axis=0, tiled=True),
        lax.all_to_all(new_values, ("heads", "sub"), split_axis=1, concat_axis=0, tiled=True),
    )
    qblocks, head_count, top_count = selection.shape
    head_size = HD
    scaling = head_size ** (-0.5)
    shaped = (qblocks, BLOCK, head_count, head_size)
    query_blocks = heads_q.reshape(shaped)
    own = own_partial(query_blocks, heads_k.reshape(shaped), heads_v.reshape(shaped), scaling)
    seq_count = lax.axis_size("seq")
    myself = lax.axis_index("seq")
    cache_blocks = cache_keys.shape[0] // BLOCK
    tile_count = cache_blocks * head_count
    request_count = qblocks * head_count * top_count
    capacity = -(-request_count // seq_count)
    requests_all = lax.all_gather(selection, "seq", axis=0, tiled=True).reshape(
        seq_count, request_count
    )
    head_of = jnp.arange(request_count) // top_count % head_count
    my_requests = selection.reshape(request_count)
    my_owner = my_requests // cache_blocks
    my_slot = my_owner * capacity + order_ranks(my_owner)
    key_tiles = cache_keys.reshape(cache_blocks, BLOCK, head_count, head_size).transpose(0, 2, 1, 3)
    value_tiles = cache_values.reshape(cache_blocks, BLOCK, head_count, head_size).transpose(
        0, 2, 1, 3
    )
    tile_set = jnp.concatenate([key_tiles, value_tiles], axis=-1).reshape(
        tile_count, BLOCK, 2 * head_size
    )
    their_owner = requests_all // cache_blocks
    local_tile = requests_all % cache_blocks * head_count + head_of[None, :]
    served = (their_owner == myself).astype(jnp.float32)
    slot_pick = one_hot(order_ranks(their_owner), capacity) * served[..., None]
    picking = jnp.einsum("erc,erl->ecl", slot_pick, one_hot(local_tile, tile_count)).astype(
        jnp.bfloat16
    )
    parts = [own]
    outgoing = jnp.einsum(
        "ecl,lkf->eckf", picking, tile_set, preferred_element_type=jnp.float32
    ).astype(jnp.bfloat16)
    incoming = lax.all_to_all(outgoing, "seq", split_axis=0, concat_axis=0, tiled=True)
    fetched = incoming.reshape(seq_count * capacity, BLOCK, 2 * head_size)[my_slot]
    fetched = fetched.reshape(qblocks, head_count, top_count, BLOCK, 2 * head_size)
    for turn in range(top_count):
        parts.append(tile_partial(query_blocks, fetched[:, :, turn], scaling))
    result = merge_parts(parts)
    result = (
        result.transpose(0, 2, 1, 3)
        .reshape(qblocks * BLOCK, head_count * head_size)
        .astype(jnp.bfloat16)
    )
    return lax.all_to_all(result, ("heads", "sub"), split_axis=0, concat_axis=1, tiled=True)


def body(queries, new_keys, new_values, cache_keys, cache_values, selection):
    qblocks, head_count, top_count = selection.shape
    blocks_total = cache_keys.shape[0] // BLOCK * lax.axis_size("seq")
    if blocks_total == top_count and qblocks == 1:
        return dense_body(queries, new_keys, new_values, cache_keys, cache_values)
    return general_body(queries, new_keys, new_values, cache_keys, cache_values, selection)


def solution(mesh):
    in_specs = (
        P(("groups", "seq", "heads", "sub"), None),
        P(("groups", "seq", "heads", "sub"), None),
        P(("groups", "seq", "heads", "sub"), None),
        P(("groups", "seq"), ("heads", "sub")),
        P(("groups", "seq"), ("heads", "sub")),
        P(("groups", "seq"), ("heads", "sub"), None),
    )
    out_specs = P(("groups", "seq", "heads", "sub"), None)
    return jax.shard_map(body, mesh=mesh, in_specs=in_specs, out_specs=out_specs, check_vma=False)
```

```python
import functools
import heapq
import math

import jax
import jax.numpy as jnp
from jax import lax
from jax.experimental import pallas as pl
from jax.experimental.pallas import tpu as pltpu
from jax.sharding import PartitionSpec as P

HD = 128
BLOCK = 512


MESH = pl.DeviceIdType.MESH
TILE = 256
KEYS = 256

READY, TAKE, PASS, START, RELAY, WORK, OWN, LOAD, FOLD, EMIT, DONE, REST = range(12)
KINDS = 16
SEND, UNIT, SPAN, MERGE, CLOSE, WIRE, HOP = 0.08, 0.78, 0.35, 0.37, 0.4, 1.43, 3.15
FIRST, EACH, LATE, DEEP = 0.81, 0.7, 20.42, 2
FAR = 2.48
K_FAR, K_OUT, K_DIST, K_OWN, W_DIST, W_SELF, W_OWN = 4.45, 10.85, -0.77, 4.61, 1.08, 7.29, 3.32


def plan_steps(count, chunks, group):
    steps = [[] for _ in range(count)]
    free = [0.0] * count
    seen, back = ([{} for _ in range(count)] for _ in range(2))
    touched, passed, worked, owned, folded, emitted, finished = (
        [set() for _ in range(count)] for _ in range(7)
    )
    wires = {(s, d): [] for s in range(count) for d in (-1, 1) if 0 <= s + d < count}
    heap = []
    for s in range(count):
        for n in range(chunks):
            seen[s][s, n] = FIRST if n % group == 0 else FAR + EACH * n
            heapq.heappush(heap, (seen[s][s, n], s))
        heapq.heappush(heap, (LATE, s))

    def first_use(s, o, n):
        if (o, n) not in touched[s]:
            touched[s].add((o, n))
            steps[s].append((READY if o == s else TAKE, o, n, 0))

    def launch(t, s, d, arrive, entry):
        finish = max([t] + wires[s, d][-1:]) + WIRE
        wires[s, d].append(finish)
        arrive[s + d][entry] = finish + HOP
        heapq.heappush(heap, (finish + HOP, s + d))
        heapq.heappush(heap, (finish, s))

    def next_send(t, s, d):
        found = []
        for (o, n), when in seen[s].items():
            onward = o == s or (o < s) == (d > 0)
            if when <= t and onward and (o, n, d) not in passed[s]:
                left = count - 1 - s if d > 0 else s
                found.append((n - K_FAR * left + (K_OWN if o == s else 0.0), 0, o, n))
        for o, n in folded[s]:
            if (o - s) * d > 0 and (o, n) not in emitted[s]:
                found.append((n + K_OUT - K_DIST * abs(o - s), 1, o, n))
        return min(found) if found else None

    def next_work(t, s):
        found = []
        for o, n in worked[s]:
            if o != s and (o, n) not in folded[s]:
                far = s + (s - o) // abs(s - o)
                if not 0 <= far < count or back[s].get((o, n), t + 1) <= t:
                    found.append((0, n - 2 * abs(o - s), FOLD, o, n, MERGE))
        for n in range(chunks):
            if (s, n) in worked[s] and n in owned[s] and n not in finished[s]:
                sides = [d for d in (-1, 1) if (s, d) in wires]
                if all(back[s].get((s, n, d), t + 1) <= t for d in sides):
                    found.append((1, n, DONE, s, n, CLOSE))
        for n in range(0, chunks, group):
            for o in range(count):
                here = all(seen[s].get((o, n + k), t + 1) <= t for k in range(group))
                if here and (o, n) not in worked[s]:
                    rank = n - (W_DIST * abs(o - s) if o != s else W_SELF)
                    found.append((2, rank, WORK, o, n, UNIT * group))
            if t >= LATE and n not in owned[s] and (s, n) in worked[s]:
                found.append((2, n + W_OWN, OWN, s, n, SPAN * group))
        return min(found) if found else None

    while heap:
        t, s = heapq.heappop(heap)
        if t < free[s] - 1e-9:
            continue
        for d in (-1, 1):
            while (s, d) in wires and sum(f > t for f in wires[s, d]) < DEEP:
                best = next_send(t, s, d)
                if best is None:
                    break
                _, out, o, n = best
                if out:
                    emitted[s].add((o, n))
                    steps[s].append((EMIT, o, n, d))
                    launch(t, s, d, back, (o, n, -d) if s + d == o else (o, n))
                else:
                    first_use(s, o, n)
                    passed[s].add((o, n, d))
                    steps[s].append((PASS, o, n, d))
                    launch(t, s, d, seen, (o, n))
                t += SEND
        best = next_work(t, s)
        free[s] = t
        if best is None:
            continue
        _, _, kind, o, n, price = best
        if kind == WORK:
            for k in range(group):
                first_use(s, o, n + k)
                worked[s].add((o, n + k))
        elif kind == OWN:
            if not owned[s]:
                steps[s].append((LOAD, o, n, 0))
            owned[s].update(range(n, n + group))
        elif kind == FOLD:
            folded[s].add((o, n))
        else:
            finished[s].add(n)
        steps[s].append((kind, o, n, 0))
        free[s] = t + price
        heapq.heappush(heap, (free[s], s))
    return steps


def join_steps(steps):
    joined = []
    for kind, o, n, d in steps:
        if kind == PASS and joined and joined[-1][1:3] == (o, n):
            if joined[-1][0] in (READY, TAKE):
                joined[-1] = (START if joined[-1][0] == READY else RELAY, o, n, d)
                continue
        joined.append((kind, o, n, d))
    return joined


def plan_codes(count, chunks, group):
    steps = plan_steps(count, chunks, group)
    codes = []
    for s, one in enumerate(steps):
        one = [x for x in one if not (x[1:3] == (s, 0) and x[0] in (READY, PASS))]
        row = [k + KINDS * ((d > 0) + 2 * (o + count * n)) for k, o, n, d in join_steps(one)]
        codes.append(row)
    base = KINDS * 2 * count * chunks
    each = max(k for k in range(1, 8) if base**k < 2**31)
    longest = -(-max(len(row) for row in codes) // each)
    words = []
    for row in codes:
        row = row + [REST] * (longest * each - len(row))
        words.append(
            [sum(row[w * each + k] * base**k for k in range(each)) for w in range(longest)]
        )
    return words, base, each


def pick_word(words, index):
    if len(words) == 1:
        return words[0]
    half = 1 << (len(words) - 1).bit_length() - 1
    low, high = words[:half], words[half:]
    return jnp.where(index >= half, pick_word(high, index - half), pick_word(low, index))


def span_tile(rows, length):
    return min(length, max(rows, TILE))


def columns(head):
    return pl.ds(pl.multiple_of(head * HD, HD), HD)


def fused_kernel(
    seq_count, heads_size, sub_size, head_count,
    q_ref, k_ref, v_ref, ck_ref, cv_ref, out_ref,
    qall, kown, vown, kc, vc, vt, msg_in, st_in, msg_out, st_out, part, pst, fin,
    loc_sem, xq_send, xq_recv, xkv_send, xkv_recv, zq_send, zq_recv,
    m_send, m_recv, t_send, t_recv, o_send, o_recv, o_loc,
):
    peers = heads_size * sub_size
    rows, span_cols = q_ref.shape[0], head_count * HD
    length = rows * peers
    tile = span_tile(rows, length)
    halves, bands = length // tile, tile // rows
    chunks = head_count * halves
    cache_blocks = kc.shape[0] // BLOCK
    scaling = HD ** (-0.5) * math.log2(math.e)
    at_seq = lax.axis_index("seq")
    place = lax.axis_index("heads") * sub_size + lax.axis_index("sub")
    has_left, has_right = at_seq > 0, at_seq < seq_count - 1

    at_heads, at_sub = lax.axis_index("heads"), lax.axis_index("sub")
    own_half = lax.div(place, bands)

    def peer_of(step):
        row = lax.rem(at_heads + step // sub_size, heads_size)
        return row * sub_size + lax.rem(at_sub + step % sub_size, sub_size)

    def half_of(chunk):
        return lax.rem(chunk + own_half, halves)

    def chunk_at(first, half):
        return first + lax.rem(half + halves - own_half, halves)

    def peer_id(peer):
        return {"heads": peer // sub_size, "sub": lax.rem(peer, sub_size)}

    def band(index):
        return pl.ds(pl.multiple_of(index * rows, rows), rows)

    def slab(index):
        return pl.ds(pl.multiple_of(index * span_cols, span_cols), span_cols)

    def head_cols(peer, head):
        return pl.ds(pl.multiple_of(peer * span_cols + head * HD, HD), HD)

    barrier = pltpu.get_barrier_semaphore()
    for step in range(1, peers):
        pl.semaphore_signal(barrier, inc=1, device_id=peer_id(peer_of(step)), device_id_type=MESH)

    @pl.when(has_left)
    def _():
        pl.semaphore_signal(barrier, inc=1, device_id={"seq": at_seq - 1}, device_id_type=MESH)

    @pl.when(has_right)
    def _():
        pl.semaphore_signal(barrier, inc=1, device_id={"seq": at_seq + 1}, device_id_type=MESH)

    own = [
        pltpu.make_async_copy(
            q_ref.at[:, slab(place)], qall.at[at_seq, band(place), :], loc_sem.at[0]
        ),
        pltpu.make_async_copy(k_ref.at[:, slab(place)], kown.at[band(place), :], loc_sem.at[1]),
        pltpu.make_async_copy(v_ref.at[:, slab(place)], vown.at[band(place), :], loc_sem.at[2]),
        pltpu.make_async_copy(ck_ref, kc, loc_sem.at[3]),
        pltpu.make_async_copy(cv_ref, vc, loc_sem.at[4]),
    ]
    for copy in (own[0], own[4], own[3], own[1], own[2]):
        copy.start()
    plans, base, each = plan_codes(seq_count, chunks, halves)
    words = []
    for index in range(len(plans[0])):
        value = jnp.int32(plans[0][index])
        for s in range(1, seq_count):
            value = jnp.where(at_seq == s, jnp.int32(plans[s][index]), value)
        words.append(value)
    sides = has_left.astype(jnp.int32) + has_right.astype(jnp.int32)
    pl.semaphore_wait(barrier, peers - 1 + sides)

    def spread_q(peer, head):
        return pltpu.make_async_remote_copy(
            src_ref=q_ref.at[:, head_cols(peer, head)],
            dst_ref=qall.at[at_seq, band(place), columns(head)],
            send_sem=xq_send.at[head, peer],
            recv_sem=xq_recv.at[head, place],
            device_id=peer_id(peer),
            device_id_type=MESH,
        )

    def landed_q(peer, head):
        return pltpu.make_async_remote_copy(
            src_ref=q_ref.at[:, head_cols(peer, head)],
            dst_ref=qall.at[at_seq, band(peer), columns(head)],
            send_sem=xq_send.at[head, peer],
            recv_sem=xq_recv.at[head, peer],
            device_id=peer_id(peer),
            device_id_type=MESH,
        )

    def spread_kv(which, peer, source):
        ref, buffer = ((k_ref, kown), (v_ref, vown))[which]
        return pltpu.make_async_remote_copy(
            src_ref=ref.at[:, slab(peer)],
            dst_ref=buffer.at[band(source), :],
            send_sem=xkv_send.at[which, peer],
            recv_sem=xkv_recv.at[which, source],
            device_id=peer_id(peer),
            device_id_type=MESH,
        )

    def span_of(chunk):
        return pl.ds(pl.multiple_of(half_of(chunk) * tile, tile), tile)

    def pass_q(owner, chunk, direction):
        piece = qall.at[owner, span_of(chunk), columns(lax.div(chunk, halves))]
        return pltpu.make_async_remote_copy(
            src_ref=piece,
            dst_ref=piece,
            send_sem=zq_send.at[direction, owner, chunk],
            recv_sem=zq_recv.at[owner, chunk],
            device_id={"seq": at_seq + 2 * direction - 1},
            device_id_type=MESH,
        )

    def pass_out(owner, head, direction):
        slot = owner + direction
        to = {"seq": at_seq + 2 * direction - 1}
        return (
            pltpu.make_async_remote_copy(
                src_ref=msg_out.at[owner, head], dst_ref=msg_in.at[slot, head],
                send_sem=m_send.at[owner, head], recv_sem=m_recv.at[slot, head],
                device_id=to, device_id_type=MESH,
            ),
            pltpu.make_async_remote_copy(
                src_ref=st_out.at[owner, head], dst_ref=st_in.at[slot, head],
                send_sem=t_send.at[owner, head], recv_sem=t_recv.at[slot, head],
                device_id=to, device_id_type=MESH,
            ),
        )

    def got_out(slot, head):
        to = {"seq": lax.rem(at_seq + 1, seq_count)}
        return (
            pltpu.make_async_remote_copy(
                src_ref=msg_out.at[0, head], dst_ref=msg_in.at[slot, head],
                send_sem=m_send.at[0, head], recv_sem=m_recv.at[slot, head],
                device_id=to, device_id_type=MESH,
            ),
            pltpu.make_async_remote_copy(
                src_ref=st_out.at[0, head], dst_ref=st_in.at[slot, head],
                send_sem=t_send.at[0, head], recv_sem=t_recv.at[slot, head],
                device_id=to, device_id_type=MESH,
            ),
        )

    def spread_out(peer, source, head):
        return pltpu.make_async_remote_copy(
            src_ref=fin.at[band(peer), columns(head)],
            dst_ref=out_ref.at[:, head_cols(source, head)],
            send_sem=o_send.at[head, peer],
            recv_sem=o_recv.at[head, source],
            device_id=peer_id(peer),
            device_id_type=MESH,
        )

    def keep_out(head):
        return pltpu.make_async_copy(
            fin.at[band(place), columns(head)],
            out_ref.at[:, head_cols(place, head)],
            o_loc.at[head],
        )

    def each_head(fn):
        pl.loop(0, head_count)(fn)

    @functools.partial(each_head)
    def _(head):
        for step in range(1, peers):
            spread_q(peer_of(step), head).start()

    for which in range(2):
        for step in range(1, peers):
            spread_kv(which, peer_of(step), place).start()

    def own_ready(chunk):
        for index in range(bands):
            peer = half_of(chunk) * bands + index

            @pl.when(peer != place)
            def _(peer=peer):
                landed_q(peer, lax.div(chunk, halves)).wait_recv()

    own[0].wait()
    own_ready(0)
    for direction, there in ((0, has_left), (1, has_right)):
        @pl.when(there)
        def _(direction=direction):
            pass_q(at_seq, 0, direction).start()

    own[4].wait()

    @functools.partial(each_head)
    def _(head):
        for block in range(cache_blocks):
            piece = vc[block * BLOCK:(block + 1) * BLOCK, columns(head)]
            vt[head, :, block * BLOCK:(block + 1) * BLOCK] = (
                piece.astype(jnp.float32).T.astype(jnp.bfloat16)
            )

    own[3].wait()

    def attend(keys, values_t, queries, causal=None):
        count = keys.shape[0] // KEYS
        scores = []
        for at in range(count):
            score = lax.dot_general(
                keys[at * KEYS:(at + 1) * KEYS],
                queries,
                (((1,), (1,)), ((), ())),
                preferred_element_type=jnp.float32,
            )
            if causal is not None:
                score = jnp.where(causal[at * KEYS:(at + 1) * KEYS], score, -jnp.inf)
            scores.append(score)
        tops = [jnp.max(score, axis=0, keepdims=True) for score in scores]
        top = functools.reduce(jnp.maximum, tops) * scaling
        mixed = total = 0.0
        for at, score in enumerate(scores):
            weights = jnp.exp2(score * scaling - top)
            total = total + jnp.sum(weights, axis=0, keepdims=True)
            mixed = mixed + jnp.dot(
                values_t[:, at * KEYS:(at + 1) * KEYS],
                weights.astype(jnp.bfloat16),
                preferred_element_type=jnp.float32,
            )
        return mixed, top, total

    def join(a, b):
        top = jnp.maximum(a[1], b[1])
        fa, fb = jnp.exp2(a[1] - top), jnp.exp2(b[1] - top)
        return a[0] * fa + b[0] * fb, top, a[2] * fa + b[2] * fb

    def put_part(owner, chunk, result):
        part[owner, chunk] = result[0]
        pst[owner, chunk, 0:1] = result[1]
        pst[owner, chunk, 1:2] = result[2]

    def get_part(owner, chunk):
        return part[owner, chunk], pst[owner, chunk, 0:1], pst[owner, chunk, 1:2]

    def cached_part(owner, chunk):
        head = lax.div(chunk, halves)
        keys, values_t = kc[:, columns(head)], vt[head]
        for at in range(halves):
            queries = qall[owner, at * tile:(at + 1) * tile, columns(head)]
            put_part(owner, chunk_at(chunk, at), attend(keys, values_t, queries))

    def own_part(chunk):
        head = lax.div(chunk, halves)
        keys = kown[:, columns(head)]
        values_t = vown[:, columns(head)].astype(jnp.float32).T.astype(jnp.bfloat16)
        for at in range(halves):
            depth = (at + 1) * tile
            key_at = lax.broadcasted_iota(jnp.int32, (depth, tile), 0)
            query_at = lax.broadcasted_iota(jnp.int32, (depth, tile), 1) + at * tile
            queries = qall[at_seq, at * tile:(at + 1) * tile, columns(head)]
            piece = attend(keys[0:depth], values_t[:, 0:depth], queries, key_at <= query_at)
            slot = chunk_at(chunk, at)
            put_part(at_seq, slot, join(piece, get_part(at_seq, slot)))

    lanes = min(tile, 128)
    folds = tile // lanes

    def fold_stats(owner, chunk, which, row):
        for index in range(folds):
            st_out[owner, chunk, which * folds + index:which * folds + index + 1] = row[
                :, index * lanes:(index + 1) * lanes
            ]

    def unfold_stats(slot, chunk, which):
        rows_of = [
            st_in[slot, chunk, which * folds + index:which * folds + index + 1]
            for index in range(folds)
        ]
        return jnp.concatenate(rows_of, axis=1)

    def take_in(slot, owner, chunk):
        for copy in got_out(slot, chunk):
            copy.wait_recv()
        mixed = msg_in[slot, chunk].astype(jnp.float32) * unfold_stats(slot, chunk, 1)
        level = unfold_stats(slot, chunk, 0)
        other = (mixed, level, jnp.ones_like(level))
        put_part(owner, chunk, join(get_part(owner, chunk), other))

    def inside(index, limit):
        return jnp.logical_and(index >= 0, index < limit)

    def foreign(index):
        distance = index // 2 + 1
        direction = lax.rem(index, 2)
        return at_seq + (2 * direction - 1) * distance, direction, distance

    def fold(owner, chunk):
        right = (owner > at_seq).astype(jnp.int32)

        @pl.when(inside(at_seq - 2 * right + 1, seq_count))
        def _():
            take_in(owner + right, owner, chunk)

        mixed = part[owner, chunk]
        total = pst[owner, chunk, 1:2]
        most = jnp.maximum(jnp.max(jnp.abs(mixed), axis=0, keepdims=True), 1e-30)
        msg_out[owner, chunk] = (
            jnp.round(mixed * (32767.0 / most)).astype(jnp.int32).astype(jnp.int16)
        )
        fold_stats(owner, chunk, 0, pst[owner, chunk, 0:1] + jnp.log2(total))
        fold_stats(owner, chunk, 1, most * (1.0 / 32767.0) / total)

    def load():
        own[1].wait()
        own[2].wait()
        for which in range(2):
            for step in range(1, peers):
                peer = peer_of(step)
                spread_kv(which, peer, peer).wait_recv()

    def close(chunk):
        head = lax.div(chunk, halves)
        for side, there in ((1, has_left), (0, has_right)):
            @pl.when(there)
            def _(side=side):
                take_in(at_seq + side, at_seq, chunk)

        done = part[at_seq, chunk] / pst[at_seq, chunk, 1:2]
        fin[span_of(chunk), columns(head)] = done.T.astype(jnp.bfloat16)
        for index in range(bands):
            peer = half_of(chunk) * bands + index

            @pl.when(peer != place)
            def _(peer=peer):
                spread_out(peer, place, head).start()

            @pl.when(peer == place)
            def _():
                keep_out(head).start()

    def emit(owner, chunk):
        for copy in pass_out(owner, chunk, (owner > at_seq).astype(jnp.int32)):
            copy.start()

    def step(code):
        kind, rest = lax.rem(code, KINDS), lax.div(code, KINDS)
        direction, rest = lax.rem(rest, 2), lax.div(rest, 2)
        owner, chunk = lax.rem(rest, seq_count), lax.div(rest, seq_count)

        @pl.when(kind <= RELAY)
        def _():
            @pl.when(jnp.logical_or(kind == READY, kind == START))
            def _():
                own_ready(chunk)

            @pl.when(jnp.logical_or(kind == TAKE, kind == RELAY))
            def _():
                pass_q(owner, chunk, 0).wait_recv()

            @pl.when(kind >= PASS)
            def _():
                pass_q(owner, chunk, direction).start()

        @pl.when(jnp.logical_and(kind > RELAY, kind < FOLD))
        def _():
            @pl.when(kind == WORK)
            def _():
                cached_part(owner, chunk)

            @pl.when(kind == OWN)
            def _():
                own_part(chunk)

            @pl.when(kind == LOAD)
            def _():
                load()

        @pl.when(kind >= FOLD)
        def _():
            @pl.when(kind == FOLD)
            def _():
                fold(owner, chunk)

            @pl.when(kind == EMIT)
            def _():
                emit(owner, chunk)

            @pl.when(kind == DONE)
            def _():
                close(chunk)

    @pl.loop(0, len(words))
    def _(index):
        word = pick_word(words, index)

        @pl.loop(0, each)
        def _(field):
            code = lax.rem(word, base)
            for k in range(1, each):
                code = jnp.where(field == k, lax.rem(lax.div(word, base**k), base), code)
            step(code)

    @functools.partial(each_head)
    def _(head):
        for step in range(1, peers):
            peer = peer_of(step)
            spread_out(peer, peer, head).wait_recv()
            spread_out(peer, place, head).wait_send()
            spread_q(peer, head).wait_send()
        keep_out(head).wait()

    @pl.loop(0, chunks)
    def _(chunk):
        for direction, there in ((0, has_left), (1, has_right)):
            @pl.when(there)
            def _(direction=direction):
                pass_q(at_seq, chunk, direction).wait_send()

        @pl.loop(0, 2 * (seq_count - 1))
        def _(index):
            owner, direction, distance = foreign(index)

            @pl.when(inside(owner, seq_count))
            def _():
                for copy in pass_out(owner, chunk, direction):
                    copy.wait_send()
                onward = 1 - direction

                @pl.when(inside(at_seq + 2 * onward - 1, seq_count))
                def _():
                    pass_q(owner, chunk, onward).wait_send()

    for which in range(2):
        for step in range(1, peers):
            spread_kv(which, peer_of(step), place).wait_send()


def dense_body(queries, new_keys, new_values, cache_keys, cache_values):
    seq_count = lax.axis_size("seq")
    heads_size, sub_size = lax.axis_size("heads"), lax.axis_size("sub")
    peers = heads_size * sub_size
    rows, width = queries.shape
    cached, span_cols = cache_keys.shape
    head_count, length = span_cols // HD, rows * peers
    tile = span_tile(rows, length)
    chunks = head_count * (length // tile)
    lanes = min(tile, 128)
    stat_rows = 2 * (tile // lanes)
    dma = pltpu.SemaphoreType.DMA
    anywhere = pl.BlockSpec(memory_space=pltpu.HBM)
    return pl.pallas_call(
        functools.partial(fused_kernel, seq_count, heads_size, sub_size, head_count),
        out_shape=jax.ShapeDtypeStruct((rows, width), jnp.bfloat16),
        in_specs=[anywhere] * 5,
        out_specs=anywhere,
        scratch_shapes=[
            pltpu.VMEM((seq_count, length, span_cols), jnp.bfloat16),
            pltpu.VMEM((length, span_cols), jnp.bfloat16),
            pltpu.VMEM((length, span_cols), jnp.bfloat16),
            pltpu.VMEM((cached, span_cols), jnp.bfloat16),
            pltpu.VMEM((cached, span_cols), jnp.bfloat16),
            pltpu.VMEM((head_count, HD, cached), jnp.bfloat16),
            pltpu.VMEM((seq_count + 1, chunks, HD, tile), jnp.int16),
            pltpu.VMEM((seq_count + 1, chunks, stat_rows, lanes), jnp.float32),
            pltpu.VMEM((seq_count, chunks, HD, tile), jnp.int16),
            pltpu.VMEM((seq_count, chunks, stat_rows, lanes), jnp.float32),
            pltpu.VMEM((seq_count, chunks, HD, tile), jnp.float32),
            pltpu.VMEM((seq_count, chunks, 8, tile), jnp.float32),
            pltpu.VMEM((length, span_cols), jnp.bfloat16),
            dma((5,)),
            dma((head_count, peers)),
            dma((head_count, peers)),
            dma((2, peers)),
            dma((2, peers)),
            dma((2, seq_count, chunks)),
            dma((seq_count, chunks)),
            dma((seq_count, chunks)),
            dma((seq_count + 1, chunks)),
            dma((seq_count, chunks)),
            dma((seq_count + 1, chunks)),
            dma((head_count, peers)),
            dma((head_count, peers)),
            dma((head_count,)),
        ],
        compiler_params=pltpu.CompilerParams(
            collective_id=0, has_side_effects=True, vmem_limit_bytes=60 * 1024 * 1024
        ),
    )(queries, new_keys, new_values, cache_keys, cache_values)


def order_ranks(owners):
    length = owners.shape[-1]
    counter = jnp.arange(length)
    earlier = counter[None, :] < counter[:, None]
    same_owner = owners[..., :, None] == owners[..., None, :]
    return jnp.sum(jnp.logical_and(same_owner, earlier), axis=-1)


def one_hot(values, length):
    return (values[..., None] == jnp.arange(length)).astype(jnp.float32)


def own_partial(query_blocks, key_blocks, value_blocks, scaling):
    scores = (
        jnp.einsum("bqhd,bkhd->bhqk", query_blocks, key_blocks, preferred_element_type=jnp.float32)
        * scaling
    )
    length = query_blocks.shape[1]
    causal = jnp.arange(length)[:, None] >= jnp.arange(length)[None, :]
    scores = jnp.where(causal, scores, -jnp.inf)
    highest = jnp.max(scores, axis=-1)
    weights = jnp.exp(scores - highest[..., None])
    totals = jnp.sum(weights, axis=-1)
    mixed = jnp.einsum(
        "bhqk,bkhd->bhqd",
        weights.astype(jnp.bfloat16),
        value_blocks,
        preferred_element_type=jnp.float32,
    )
    return (mixed, highest, totals)


def tile_partial(query_blocks, tile_pair, scaling):
    head_size = query_blocks.shape[-1]
    scores = (
        jnp.einsum(
            "bqhd,bhkd->bhqk",
            query_blocks,
            tile_pair[..., :head_size],
            preferred_element_type=jnp.float32,
        )
        * scaling
    )
    highest = jnp.max(scores, axis=-1)
    weights = jnp.exp(scores - highest[..., None])
    totals = jnp.sum(weights, axis=-1)
    mixed = jnp.einsum(
        "bhqk,bhkd->bhqd",
        weights.astype(jnp.bfloat16),
        tile_pair[..., head_size:],
        preferred_element_type=jnp.float32,
    )
    return (mixed, highest, totals)


def merge_parts(parts):
    top = parts[0][1]
    for part in parts[1:]:
        top = jnp.maximum(top, part[1])
    numer = jnp.zeros(parts[0][0].shape, jnp.float32)
    denom = jnp.zeros(parts[0][2].shape, jnp.float32)
    for part in parts:
        factor = jnp.exp(part[1] - top)
        numer = numer + factor[..., None] * part[0]
        denom = denom + factor * part[2]
    return numer / denom[..., None]


def general_body(queries, new_keys, new_values, cache_keys, cache_values, selection):
    heads_q, heads_k, heads_v = (
        lax.all_to_all(queries, ("heads", "sub"), split_axis=1, concat_axis=0, tiled=True),
        lax.all_to_all(new_keys, ("heads", "sub"), split_axis=1, concat_axis=0, tiled=True),
        lax.all_to_all(new_values, ("heads", "sub"), split_axis=1, concat_axis=0, tiled=True),
    )
    qblocks, head_count, top_count = selection.shape
    head_size = HD
    scaling = head_size ** (-0.5)
    shaped = (qblocks, BLOCK, head_count, head_size)
    query_blocks = heads_q.reshape(shaped)
    own = own_partial(query_blocks, heads_k.reshape(shaped), heads_v.reshape(shaped), scaling)
    seq_count = lax.axis_size("seq")
    myself = lax.axis_index("seq")
    cache_blocks = cache_keys.shape[0] // BLOCK
    tile_count = cache_blocks * head_count
    request_count = qblocks * head_count * top_count
    capacity = -(-request_count // seq_count)
    requests_all = lax.all_gather(selection, "seq", axis=0, tiled=True).reshape(
        seq_count, request_count
    )
    head_of = jnp.arange(request_count) // top_count % head_count
    my_requests = selection.reshape(request_count)
    my_owner = my_requests // cache_blocks
    my_slot = my_owner * capacity + order_ranks(my_owner)
    key_tiles = cache_keys.reshape(cache_blocks, BLOCK, head_count, head_size).transpose(0, 2, 1, 3)
    value_tiles = cache_values.reshape(cache_blocks, BLOCK, head_count, head_size).transpose(
        0, 2, 1, 3
    )
    tile_set = jnp.concatenate([key_tiles, value_tiles], axis=-1).reshape(
        tile_count, BLOCK, 2 * head_size
    )
    their_owner = requests_all // cache_blocks
    local_tile = requests_all % cache_blocks * head_count + head_of[None, :]
    served = (their_owner == myself).astype(jnp.float32)
    slot_pick = one_hot(order_ranks(their_owner), capacity) * served[..., None]
    picking = jnp.einsum("erc,erl->ecl", slot_pick, one_hot(local_tile, tile_count)).astype(
        jnp.bfloat16
    )
    parts = [own]
    outgoing = jnp.einsum(
        "ecl,lkf->eckf", picking, tile_set, preferred_element_type=jnp.float32
    ).astype(jnp.bfloat16)
    incoming = lax.all_to_all(outgoing, "seq", split_axis=0, concat_axis=0, tiled=True)
    fetched = incoming.reshape(seq_count * capacity, BLOCK, 2 * head_size)[my_slot]
    fetched = fetched.reshape(qblocks, head_count, top_count, BLOCK, 2 * head_size)
    for turn in range(top_count):
        parts.append(tile_partial(query_blocks, fetched[:, :, turn], scaling))
    result = merge_parts(parts)
    result = (
        result.transpose(0, 2, 1, 3)
        .reshape(qblocks * BLOCK, head_count * head_size)
        .astype(jnp.bfloat16)
    )
    return lax.all_to_all(result, ("heads", "sub"), split_axis=0, concat_axis=1, tiled=True)


def body(queries, new_keys, new_values, cache_keys, cache_values, selection):
    qblocks, head_count, top_count = selection.shape
    blocks_total = cache_keys.shape[0] // BLOCK * lax.axis_size("seq")
    if blocks_total == top_count and qblocks == 1:
        return dense_body(queries, new_keys, new_values, cache_keys, cache_values)
    return general_body(queries, new_keys, new_values, cache_keys, cache_values, selection)


def solution(mesh):
    in_specs = (
        P(("groups", "seq", "heads", "sub"), None),
        P(("groups", "seq", "heads", "sub"), None),
        P(("groups", "seq", "heads", "sub"), None),
        P(("groups", "seq"), ("heads", "sub")),
        P(("groups", "seq"), ("heads", "sub")),
        P(("groups", "seq"), ("heads", "sub"), None),
    )
    out_specs = P(("groups", "seq", "heads", "sub"), None)
    return jax.shard_map(body, mesh=mesh, in_specs=in_specs, out_specs=out_specs, check_vma=False)
```

```python
import functools
import heapq
import math

import jax
import jax.numpy as jnp
from jax import lax
from jax.experimental import pallas as pl
from jax.experimental.pallas import tpu as pltpu
from jax.sharding import PartitionSpec as P

HD = 128
BLOCK = 512


MESH = pl.DeviceIdType.MESH
TILE = 256
KEYS = 256

READY, TAKE, PASS, START, RELAY, WORK, OWN, LOAD, FOLD, EMIT, DONE, REST = range(12)
KINDS = 16
SEND, UNIT, SPAN, MERGE, CLOSE, WIRE, HOP = 0.08, 0.78, 0.35, 0.37, 0.4, 1.43, 3.15
FIRST, EACH, LATE, DEEP = 0.81, 0.7, 20.42, 2
FAR = 2.48
K_FAR, K_OUT, K_DIST, K_OWN, W_DIST, W_SELF, W_OWN = 4.45, 10.85, -0.77, 4.61, 1.08, 7.29, 3.32


def plan_steps(count, chunks, group):
    steps = [[] for _ in range(count)]
    free = [0.0] * count
    seen, back = ([{} for _ in range(count)] for _ in range(2))
    touched, passed, worked, owned, folded, emitted, finished = (
        [set() for _ in range(count)] for _ in range(7)
    )
    wires = {(s, d): [] for s in range(count) for d in (-1, 1) if 0 <= s + d < count}
    heap = []
    for s in range(count):
        for n in range(chunks):
            seen[s][s, n] = FIRST if n % group == 0 else FAR + EACH * n
            heapq.heappush(heap, (seen[s][s, n], s))
        heapq.heappush(heap, (LATE, s))

    def first_use(s, o, n):
        if (o, n) not in touched[s]:
            touched[s].add((o, n))
            steps[s].append((READY if o == s else TAKE, o, n, 0))

    def launch(t, s, d, arrive, entry):
        finish = max([t] + wires[s, d][-1:]) + WIRE
        wires[s, d].append(finish)
        arrive[s + d][entry] = finish + HOP
        heapq.heappush(heap, (finish + HOP, s + d))
        heapq.heappush(heap, (finish, s))

    def next_send(t, s, d):
        found = []
        for (o, n), when in seen[s].items():
            onward = o == s or (o < s) == (d > 0)
            if when <= t and onward and (o, n, d) not in passed[s]:
                left = count - 1 - s if d > 0 else s
                found.append((n - K_FAR * left + (K_OWN if o == s else 0.0), 0, o, n))
        for o, n in folded[s]:
            if (o - s) * d > 0 and (o, n) not in emitted[s]:
                found.append((n + K_OUT - K_DIST * abs(o - s), 1, o, n))
        return min(found) if found else None

    def next_work(t, s):
        found = []
        for o, n in worked[s]:
            if o != s and (o, n) not in folded[s]:
                far = s + (s - o) // abs(s - o)
                if not 0 <= far < count or back[s].get((o, n), t + 1) <= t:
                    found.append((0, n - 2 * abs(o - s), FOLD, o, n, MERGE))
        for n in range(chunks):
            if (s, n) in worked[s] and n in owned[s] and n not in finished[s]:
                sides = [d for d in (-1, 1) if (s, d) in wires]
                if all(back[s].get((s, n, d), t + 1) <= t for d in sides):
                    found.append((1, n, DONE, s, n, CLOSE))
        for n in range(0, chunks, group):
            for o in range(count):
                here = all(seen[s].get((o, n + k), t + 1) <= t for k in range(group))
                if here and (o, n) not in worked[s]:
                    rank = n - (W_DIST * abs(o - s) if o != s else W_SELF)
                    found.append((2, rank, WORK, o, n, UNIT * group))
            if t >= LATE and n not in owned[s] and (s, n) in worked[s]:
                found.append((2, n + W_OWN, OWN, s, n, SPAN * group))
        return min(found) if found else None

    while heap:
        t, s = heapq.heappop(heap)
        if t < free[s] - 1e-9:
            continue
        for d in (-1, 1):
            while (s, d) in wires and sum(f > t for f in wires[s, d]) < DEEP:
                best = next_send(t, s, d)
                if best is None:
                    break
                _, out, o, n = best
                if out:
                    emitted[s].add((o, n))
                    steps[s].append((EMIT, o, n, d))
                    launch(t, s, d, back, (o, n, -d) if s + d == o else (o, n))
                else:
                    first_use(s, o, n)
                    passed[s].add((o, n, d))
                    steps[s].append((PASS, o, n, d))
                    launch(t, s, d, seen, (o, n))
                t += SEND
        best = next_work(t, s)
        free[s] = t
        if best is None:
            continue
        _, _, kind, o, n, price = best
        if kind == WORK:
            for k in range(group):
                first_use(s, o, n + k)
                worked[s].add((o, n + k))
        elif kind == OWN:
            if not owned[s]:
                steps[s].append((LOAD, o, n, 0))
            owned[s].update(range(n, n + group))
        elif kind == FOLD:
            folded[s].add((o, n))
        else:
            finished[s].add(n)
        steps[s].append((kind, o, n, 0))
        free[s] = t + price
        heapq.heappush(heap, (free[s], s))
    return steps


def join_steps(steps):
    joined = []
    for kind, o, n, d in steps:
        if kind == PASS and joined and joined[-1][1:3] == (o, n):
            if joined[-1][0] in (READY, TAKE):
                joined[-1] = (START if joined[-1][0] == READY else RELAY, o, n, d)
                continue
        joined.append((kind, o, n, d))
    return joined


def plan_codes(count, chunks, group):
    steps = plan_steps(count, chunks, group)
    codes = []
    for s, one in enumerate(steps):
        one = [x for x in one if not (x[1:3] == (s, 0) and x[0] in (READY, PASS))]
        row = [k + KINDS * ((d > 0) + 2 * (o + count * n)) for k, o, n, d in join_steps(one)]
        codes.append(row)
    base = KINDS * 2 * count * chunks
    each = max(k for k in range(1, 8) if base**k < 2**31)
    longest = -(-max(len(row) for row in codes) // each)
    words = []
    for row in codes:
        row = row + [REST] * (longest * each - len(row))
        words.append(
            [sum(row[w * each + k] * base**k for k in range(each)) for w in range(longest)]
        )
    return words, base, each


def pick_word(words, index):
    if len(words) == 1:
        return words[0]
    half = 1 << (len(words) - 1).bit_length() - 1
    low, high = words[:half], words[half:]
    return jnp.where(index >= half, pick_word(high, index - half), pick_word(low, index))


def span_tile(rows, length):
    return min(length, max(rows, TILE))


def columns(head):
    return pl.ds(pl.multiple_of(head * HD, HD), HD)


def fused_kernel(
    seq_count, heads_size, sub_size, head_count,
    q_ref, k_ref, v_ref, ck_ref, cv_ref, out_ref,
    qall, kown, vown, kc, vc, vt, msg_in, st_in, msg_out, st_out, part, pst, fin,
    loc_sem, xq_send, xq_recv, xkv_send, xkv_recv, zq_send, zq_recv,
    m_send, m_recv, t_send, t_recv, o_send, o_recv, o_loc,
):
    peers = heads_size * sub_size
    rows, span_cols = q_ref.shape[0], head_count * HD
    length = rows * peers
    tile = span_tile(rows, length)
    halves, bands = length // tile, tile // rows
    chunks = head_count * halves
    cache_blocks = kc.shape[0] // BLOCK
    scaling = HD ** (-0.5) * math.log2(math.e)
    at_seq = lax.axis_index("seq")
    place = lax.axis_index("heads") * sub_size + lax.axis_index("sub")
    has_left, has_right = at_seq > 0, at_seq < seq_count - 1

    at_heads, at_sub = lax.axis_index("heads"), lax.axis_index("sub")
    own_half = lax.div(place, bands)

    def peer_of(step):
        row = lax.rem(at_heads + step // sub_size, heads_size)
        return row * sub_size + lax.rem(at_sub + step % sub_size, sub_size)

    def half_of(chunk):
        return lax.rem(chunk + own_half, halves)

    def chunk_at(first, half):
        return first + lax.rem(half + halves - own_half, halves)

    def peer_id(peer):
        return {"heads": peer // sub_size, "sub": lax.rem(peer, sub_size)}

    def band(index):
        return pl.ds(pl.multiple_of(index * rows, rows), rows)

    def slab(index):
        return pl.ds(pl.multiple_of(index * span_cols, span_cols), span_cols)

    def head_cols(peer, head):
        return pl.ds(pl.multiple_of(peer * span_cols + head * HD, HD), HD)

    barrier = pltpu.get_barrier_semaphore()
    for step in range(1, peers):
        pl.semaphore_signal(barrier, inc=1, device_id=peer_id(peer_of(step)), device_id_type=MESH)

    @pl.when(has_left)
    def _():
        pl.semaphore_signal(barrier, inc=1, device_id={"seq": at_seq - 1}, device_id_type=MESH)

    @pl.when(has_right)
    def _():
        pl.semaphore_signal(barrier, inc=1, device_id={"seq": at_seq + 1}, device_id_type=MESH)

    own = [
        pltpu.make_async_copy(
            q_ref.at[:, slab(place)], qall.at[at_seq, band(place), :], loc_sem.at[0]
        ),
        pltpu.make_async_copy(k_ref.at[:, slab(place)], kown.at[band(place), :], loc_sem.at[1]),
        pltpu.make_async_copy(v_ref.at[:, slab(place)], vown.at[band(place), :], loc_sem.at[2]),
        pltpu.make_async_copy(ck_ref, kc, loc_sem.at[3]),
        pltpu.make_async_copy(cv_ref, vc, loc_sem.at[4]),
    ]
    for copy in (own[0], own[4], own[3], own[1], own[2]):
        copy.start()
    plans, base, each = plan_codes(seq_count, chunks, halves)
    words = []
    for index in range(len(plans[0])):
        value = jnp.int32(plans[0][index])
        for s in range(1, seq_count):
            value = jnp.where(at_seq == s, jnp.int32(plans[s][index]), value)
        words.append(value)
    sides = has_left.astype(jnp.int32) + has_right.astype(jnp.int32)
    pl.semaphore_wait(barrier, peers - 1 + sides)

    def spread_q(peer, head):
        return pltpu.make_async_remote_copy(
            src_ref=q_ref.at[:, head_cols(peer, head)],
            dst_ref=qall.at[at_seq, band(place), columns(head)],
            send_sem=xq_send.at[head, peer],
            recv_sem=xq_recv.at[head, place],
            device_id=peer_id(peer),
            device_id_type=MESH,
        )

    def landed_q(peer, head):
        return pltpu.make_async_remote_copy(
            src_ref=q_ref.at[:, head_cols(peer, head)],
            dst_ref=qall.at[at_seq, band(peer), columns(head)],
            send_sem=xq_send.at[head, peer],
            recv_sem=xq_recv.at[head, peer],
            device_id=peer_id(peer),
            device_id_type=MESH,
        )

    def spread_kv(which, peer, source):
        ref, buffer = ((k_ref, kown), (v_ref, vown))[which]
        return pltpu.make_async_remote_copy(
            src_ref=ref.at[:, slab(peer)],
            dst_ref=buffer.at[band(source), :],
            send_sem=xkv_send.at[which, peer],
            recv_sem=xkv_recv.at[which, source],
            device_id=peer_id(peer),
            device_id_type=MESH,
        )

    def span_of(chunk):
        return pl.ds(pl.multiple_of(half_of(chunk) * tile, tile), tile)

    def pass_q(owner, chunk, direction):
        piece = qall.at[owner, span_of(chunk), columns(lax.div(chunk, halves))]
        return pltpu.make_async_remote_copy(
            src_ref=piece,
            dst_ref=piece,
            send_sem=zq_send.at[direction, owner, chunk],
            recv_sem=zq_recv.at[owner, chunk],
            device_id={"seq": at_seq + 2 * direction - 1},
            device_id_type=MESH,
        )

    def pass_out(owner, head, direction):
        slot = owner + direction
        to = {"seq": at_seq + 2 * direction - 1}
        return (
            pltpu.make_async_remote_copy(
                src_ref=msg_out.at[owner, head], dst_ref=msg_in.at[slot, head],
                send_sem=m_send.at[owner, head], recv_sem=m_recv.at[slot, head],
                device_id=to, device_id_type=MESH,
            ),
            pltpu.make_async_remote_copy(
                src_ref=st_out.at[owner, head], dst_ref=st_in.at[slot, head],
                send_sem=t_send.at[owner, head], recv_sem=t_recv.at[slot, head],
                device_id=to, device_id_type=MESH,
            ),
        )

    def got_out(slot, head):
        to = {"seq": lax.rem(at_seq + 1, seq_count)}
        return (
            pltpu.make_async_remote_copy(
                src_ref=msg_out.at[0, head], dst_ref=msg_in.at[slot, head],
                send_sem=m_send.at[0, head], recv_sem=m_recv.at[slot, head],
                device_id=to, device_id_type=MESH,
            ),
            pltpu.make_async_remote_copy(
                src_ref=st_out.at[0, head], dst_ref=st_in.at[slot, head],
                send_sem=t_send.at[0, head], recv_sem=t_recv.at[slot, head],
                device_id=to, device_id_type=MESH,
            ),
        )

    def spread_out(peer, source, head):
        return pltpu.make_async_remote_copy(
            src_ref=fin.at[band(peer), columns(head)],
            dst_ref=out_ref.at[:, head_cols(source, head)],
            send_sem=o_send.at[head, peer],
            recv_sem=o_recv.at[head, source],
            device_id=peer_id(peer),
            device_id_type=MESH,
        )

    def keep_out(head):
        return pltpu.make_async_copy(
            fin.at[band(place), columns(head)],
            out_ref.at[:, head_cols(place, head)],
            o_loc.at[head],
        )

    def each_head(fn):
        pl.loop(0, head_count)(fn)

    @functools.partial(each_head)
    def _(head):
        for step in range(1, peers):
            spread_q(peer_of(step), head).start()

    for which in range(2):
        for step in range(1, peers):
            spread_kv(which, peer_of(step), place).start()

    def own_ready(chunk):
        for index in range(bands):
            peer = half_of(chunk) * bands + index

            @pl.when(peer != place)
            def _(peer=peer):
                landed_q(peer, lax.div(chunk, halves)).wait_recv()

    own[0].wait()
    own_ready(0)
    for direction, there in ((0, has_left), (1, has_right)):
        @pl.when(there)
        def _(direction=direction):
            pass_q(at_seq, 0, direction).start()

    own[4].wait()

    @functools.partial(each_head)
    def _(head):
        for block in range(cache_blocks):
            piece = vc[block * BLOCK:(block + 1) * BLOCK, columns(head)]
            vt[head, :, block * BLOCK:(block + 1) * BLOCK] = (
                piece.astype(jnp.float32).T.astype(jnp.bfloat16)
            )

    own[3].wait()

    def attend(keys, values_t, queries, causal=None):
        count = keys.shape[0] // KEYS
        scores = []
        for at in range(count):
            score = lax.dot_general(
                keys[at * KEYS:(at + 1) * KEYS],
                queries,
                (((1,), (1,)), ((), ())),
                preferred_element_type=jnp.float32,
            )
            if causal is not None:
                score = jnp.where(causal[at * KEYS:(at + 1) * KEYS], score, -jnp.inf)
            scores.append(score)
        tops = [jnp.max(score, axis=0, keepdims=True) for score in scores]
        top = functools.reduce(jnp.maximum, tops) * scaling
        mixed = total = 0.0
        for at, score in enumerate(scores):
            weights = jnp.exp2(score * scaling - top)
            total = total + jnp.sum(weights, axis=0, keepdims=True)
            mixed = mixed + jnp.dot(
                values_t[:, at * KEYS:(at + 1) * KEYS],
                weights.astype(jnp.bfloat16),
                preferred_element_type=jnp.float32,
            )
        return mixed, top, total

    def join(a, b):
        top = jnp.maximum(a[1], b[1])
        fa, fb = jnp.exp2(a[1] - top), jnp.exp2(b[1] - top)
        return a[0] * fa + b[0] * fb, top, a[2] * fa + b[2] * fb

    def put_part(owner, chunk, result):
        part[owner, chunk] = result[0]
        pst[owner, chunk, 0:1] = result[1]
        pst[owner, chunk, 1:2] = result[2]

    def get_part(owner, chunk):
        return part[owner, chunk], pst[owner, chunk, 0:1], pst[owner, chunk, 1:2]

    def cached_part(owner, chunk):
        head = lax.div(chunk, halves)
        keys, values_t = kc[:, columns(head)], vt[head]
        for at in range(halves):
            queries = qall[owner, at * tile:(at + 1) * tile, columns(head)]
            put_part(owner, chunk_at(chunk, at), attend(keys, values_t, queries))

    def own_part(chunk):
        head = lax.div(chunk, halves)
        keys = kown[:, columns(head)]
        values_t = vown[:, columns(head)].astype(jnp.float32).T.astype(jnp.bfloat16)
        for at in range(halves):
            depth = (at + 1) * tile
            key_at = lax.broadcasted_iota(jnp.int32, (depth, tile), 0)
            query_at = lax.broadcasted_iota(jnp.int32, (depth, tile), 1) + at * tile
            queries = qall[at_seq, at * tile:(at + 1) * tile, columns(head)]
            piece = attend(keys[0:depth], values_t[:, 0:depth], queries, key_at <= query_at)
            slot = chunk_at(chunk, at)
            put_part(at_seq, slot, join(piece, get_part(at_seq, slot)))

    lanes = min(tile, 128)
    folds = tile // lanes

    def fold_stats(owner, chunk, which, row):
        for index in range(folds):
            st_out[owner, chunk, which * folds + index:which * folds + index + 1] = row[
                :, index * lanes:(index + 1) * lanes
            ]

    def unfold_stats(slot, chunk, which):
        rows_of = [
            st_in[slot, chunk, which * folds + index:which * folds + index + 1]
            for index in range(folds)
        ]
        return jnp.concatenate(rows_of, axis=1)

    def take_in(slot, owner, chunk):
        for copy in got_out(slot, chunk):
            copy.wait_recv()
        mixed = msg_in[slot, chunk].astype(jnp.float32) * unfold_stats(slot, chunk, 1)
        level = unfold_stats(slot, chunk, 0)
        other = (mixed, level, jnp.ones_like(level))
        put_part(owner, chunk, join(get_part(owner, chunk), other))

    def inside(index, limit):
        return jnp.logical_and(index >= 0, index < limit)

    def foreign(index):
        distance = index // 2 + 1
        direction = lax.rem(index, 2)
        return at_seq + (2 * direction - 1) * distance, direction, distance

    def fold(owner, chunk):
        right = (owner > at_seq).astype(jnp.int32)

        @pl.when(inside(at_seq - 2 * right + 1, seq_count))
        def _():
            take_in(owner + right, owner, chunk)

        mixed = part[owner, chunk]
        total = pst[owner, chunk, 1:2]
        most = jnp.maximum(jnp.max(jnp.abs(mixed), axis=0, keepdims=True), 1e-30)
        msg_out[owner, chunk] = (
            jnp.round(mixed * (32767.0 / most)).astype(jnp.int32).astype(jnp.int16)
        )
        fold_stats(owner, chunk, 0, pst[owner, chunk, 0:1] + jnp.log2(total))
        fold_stats(owner, chunk, 1, most * (1.0 / 32767.0) / total)

    def load():
        own[1].wait()
        own[2].wait()
        for which in range(2):
            for step in range(1, peers):
                peer = peer_of(step)
                spread_kv(which, peer, peer).wait_recv()

    def close(chunk):
        head = lax.div(chunk, halves)
        for side, there in ((1, has_left), (0, has_right)):
            @pl.when(there)
            def _(side=side):
                take_in(at_seq + side, at_seq, chunk)

        done = part[at_seq, chunk] / pst[at_seq, chunk, 1:2]
        fin[span_of(chunk), columns(head)] = done.T.astype(jnp.bfloat16)
        for index in range(bands):
            peer = half_of(chunk) * bands + index

            @pl.when(peer != place)
            def _(peer=peer):
                spread_out(peer, place, head).start()

            @pl.when(peer == place)
            def _():
                keep_out(head).start()

    def emit(owner, chunk):
        for copy in pass_out(owner, chunk, (owner > at_seq).astype(jnp.int32)):
            copy.start()

    def step(code):
        kind, rest = lax.rem(code, KINDS), lax.div(code, KINDS)
        direction, rest = lax.rem(rest, 2), lax.div(rest, 2)
        owner, chunk = lax.rem(rest, seq_count), lax.div(rest, seq_count)

        @pl.when(kind <= RELAY)
        def _():
            @pl.when(jnp.logical_or(kind == READY, kind == START))
            def _():
                own_ready(chunk)

            @pl.when(jnp.logical_or(kind == TAKE, kind == RELAY))
            def _():
                pass_q(owner, chunk, 0).wait_recv()

            @pl.when(kind >= PASS)
            def _():
                pass_q(owner, chunk, direction).start()

        @pl.when(jnp.logical_and(kind > RELAY, kind < FOLD))
        def _():
            @pl.when(kind == WORK)
            def _():
                cached_part(owner, chunk)

            @pl.when(kind == OWN)
            def _():
                own_part(chunk)

            @pl.when(kind == LOAD)
            def _():
                load()

        @pl.when(kind >= FOLD)
        def _():
            @pl.when(kind == FOLD)
            def _():
                fold(owner, chunk)

            @pl.when(kind == EMIT)
            def _():
                emit(owner, chunk)

            @pl.when(kind == DONE)
            def _():
                close(chunk)

    @pl.loop(0, len(words))
    def _(index):
        word = pick_word(words, index)

        @pl.loop(0, each)
        def _(field):
            code = lax.rem(word, base)
            for k in range(1, each):
                code = jnp.where(field == k, lax.rem(lax.div(word, base**k), base), code)
            step(code)

    @pl.loop(0, chunks)
    def _(chunk):
        for direction, there in ((0, has_left), (1, has_right)):
            @pl.when(there)
            def _(direction=direction):
                pass_q(at_seq, chunk, direction).wait_send()

        @pl.loop(0, 2 * (seq_count - 1))
        def _(index):
            owner, direction, distance = foreign(index)

            @pl.when(inside(owner, seq_count))
            def _():
                for copy in pass_out(owner, chunk, direction):
                    copy.wait_send()
                onward = 1 - direction

                @pl.when(inside(at_seq + 2 * onward - 1, seq_count))
                def _():
                    pass_q(owner, chunk, onward).wait_send()

    for which in range(2):
        for step in range(1, peers):
            spread_kv(which, peer_of(step), place).wait_send()

    @functools.partial(each_head)
    def _(head):
        for step in range(1, peers):
            spread_q(peer_of(step), head).wait_send()

    @functools.partial(each_head)
    def _(head):
        for step in range(1, peers):
            peer = peer_of(step)
            spread_out(peer, peer, head).wait_recv()
            spread_out(peer, place, head).wait_send()
        keep_out(head).wait()


def dense_body(queries, new_keys, new_values, cache_keys, cache_values):
    seq_count = lax.axis_size("seq")
    heads_size, sub_size = lax.axis_size("heads"), lax.axis_size("sub")
    peers = heads_size * sub_size
    rows, width = queries.shape
    cached, span_cols = cache_keys.shape
    head_count, length = span_cols // HD, rows * peers
    tile = span_tile(rows, length)
    chunks = head_count * (length // tile)
    lanes = min(tile, 128)
    stat_rows = 2 * (tile // lanes)
    dma = pltpu.SemaphoreType.DMA
    anywhere = pl.BlockSpec(memory_space=pltpu.HBM)
    return pl.pallas_call(
        functools.partial(fused_kernel, seq_count, heads_size, sub_size, head_count),
        out_shape=jax.ShapeDtypeStruct((rows, width), jnp.bfloat16),
        in_specs=[anywhere] * 5,
        out_specs=anywhere,
        scratch_shapes=[
            pltpu.VMEM((seq_count, length, span_cols), jnp.bfloat16),
            pltpu.VMEM((length, span_cols), jnp.bfloat16),
            pltpu.VMEM((length, span_cols), jnp.bfloat16),
            pltpu.VMEM((cached, span_cols), jnp.bfloat16),
            pltpu.VMEM((cached, span_cols), jnp.bfloat16),
            pltpu.VMEM((head_count, HD, cached), jnp.bfloat16),
            pltpu.VMEM((seq_count + 1, chunks, HD, tile), jnp.int16),
            pltpu.VMEM((seq_count + 1, chunks, stat_rows, lanes), jnp.float32),
            pltpu.VMEM((seq_count, chunks, HD, tile), jnp.int16),
            pltpu.VMEM((seq_count, chunks, stat_rows, lanes), jnp.float32),
            pltpu.VMEM((seq_count, chunks, HD, tile), jnp.float32),
            pltpu.VMEM((seq_count, chunks, 8, tile), jnp.float32),
            pltpu.VMEM((length, span_cols), jnp.bfloat16),
            dma((5,)),
            dma((head_count, peers)),
            dma((head_count, peers)),
            dma((2, peers)),
            dma((2, peers)),
            dma((2, seq_count, chunks)),
            dma((seq_count, chunks)),
            dma((seq_count, chunks)),
            dma((seq_count + 1, chunks)),
            dma((seq_count, chunks)),
            dma((seq_count + 1, chunks)),
            dma((head_count, peers)),
            dma((head_count, peers)),
            dma((head_count,)),
        ],
        compiler_params=pltpu.CompilerParams(
            collective_id=0, has_side_effects=True, vmem_limit_bytes=60 * 1024 * 1024
        ),
    )(queries, new_keys, new_values, cache_keys, cache_values)


def order_ranks(owners):
    length = owners.shape[-1]
    counter = jnp.arange(length)
    earlier = counter[None, :] < counter[:, None]
    same_owner = owners[..., :, None] == owners[..., None, :]
    return jnp.sum(jnp.logical_and(same_owner, earlier), axis=-1)


def one_hot(values, length):
    return (values[..., None] == jnp.arange(length)).astype(jnp.float32)


def own_partial(query_blocks, key_blocks, value_blocks, scaling):
    scores = (
        jnp.einsum("bqhd,bkhd->bhqk", query_blocks, key_blocks, preferred_element_type=jnp.float32)
        * scaling
    )
    length = query_blocks.shape[1]
    causal = jnp.arange(length)[:, None] >= jnp.arange(length)[None, :]
    scores = jnp.where(causal, scores, -jnp.inf)
    highest = jnp.max(scores, axis=-1)
    weights = jnp.exp(scores - highest[..., None])
    totals = jnp.sum(weights, axis=-1)
    mixed = jnp.einsum(
        "bhqk,bkhd->bhqd",
        weights.astype(jnp.bfloat16),
        value_blocks,
        preferred_element_type=jnp.float32,
    )
    return (mixed, highest, totals)


def tile_partial(query_blocks, tile_pair, scaling):
    head_size = query_blocks.shape[-1]
    scores = (
        jnp.einsum(
            "bqhd,bhkd->bhqk",
            query_blocks,
            tile_pair[..., :head_size],
            preferred_element_type=jnp.float32,
        )
        * scaling
    )
    highest = jnp.max(scores, axis=-1)
    weights = jnp.exp(scores - highest[..., None])
    totals = jnp.sum(weights, axis=-1)
    mixed = jnp.einsum(
        "bhqk,bhkd->bhqd",
        weights.astype(jnp.bfloat16),
        tile_pair[..., head_size:],
        preferred_element_type=jnp.float32,
    )
    return (mixed, highest, totals)


def merge_parts(parts):
    top = parts[0][1]
    for part in parts[1:]:
        top = jnp.maximum(top, part[1])
    numer = jnp.zeros(parts[0][0].shape, jnp.float32)
    denom = jnp.zeros(parts[0][2].shape, jnp.float32)
    for part in parts:
        factor = jnp.exp(part[1] - top)
        numer = numer + factor[..., None] * part[0]
        denom = denom + factor * part[2]
    return numer / denom[..., None]


def general_body(queries, new_keys, new_values, cache_keys, cache_values, selection):
    heads_q, heads_k, heads_v = (
        lax.all_to_all(queries, ("heads", "sub"), split_axis=1, concat_axis=0, tiled=True),
        lax.all_to_all(new_keys, ("heads", "sub"), split_axis=1, concat_axis=0, tiled=True),
        lax.all_to_all(new_values, ("heads", "sub"), split_axis=1, concat_axis=0, tiled=True),
    )
    qblocks, head_count, top_count = selection.shape
    head_size = HD
    scaling = head_size ** (-0.5)
    shaped = (qblocks, BLOCK, head_count, head_size)
    query_blocks = heads_q.reshape(shaped)
    own = own_partial(query_blocks, heads_k.reshape(shaped), heads_v.reshape(shaped), scaling)
    seq_count = lax.axis_size("seq")
    myself = lax.axis_index("seq")
    cache_blocks = cache_keys.shape[0] // BLOCK
    tile_count = cache_blocks * head_count
    request_count = qblocks * head_count * top_count
    capacity = -(-request_count // seq_count)
    requests_all = lax.all_gather(selection, "seq", axis=0, tiled=True).reshape(
        seq_count, request_count
    )
    head_of = jnp.arange(request_count) // top_count % head_count
    my_requests = selection.reshape(request_count)
    my_owner = my_requests // cache_blocks
    my_slot = my_owner * capacity + order_ranks(my_owner)
    key_tiles = cache_keys.reshape(cache_blocks, BLOCK, head_count, head_size).transpose(0, 2, 1, 3)
    value_tiles = cache_values.reshape(cache_blocks, BLOCK, head_count, head_size).transpose(
        0, 2, 1, 3
    )
    tile_set = jnp.concatenate([key_tiles, value_tiles], axis=-1).reshape(
        tile_count, BLOCK, 2 * head_size
    )
    their_owner = requests_all // cache_blocks
    local_tile = requests_all % cache_blocks * head_count + head_of[None, :]
    served = (their_owner == myself).astype(jnp.float32)
    slot_pick = one_hot(order_ranks(their_owner), capacity) * served[..., None]
    picking = jnp.einsum("erc,erl->ecl", slot_pick, one_hot(local_tile, tile_count)).astype(
        jnp.bfloat16
    )
    parts = [own]
    outgoing = jnp.einsum(
        "ecl,lkf->eckf", picking, tile_set, preferred_element_type=jnp.float32
    ).astype(jnp.bfloat16)
    incoming = lax.all_to_all(outgoing, "seq", split_axis=0, concat_axis=0, tiled=True)
    fetched = incoming.reshape(seq_count * capacity, BLOCK, 2 * head_size)[my_slot]
    fetched = fetched.reshape(qblocks, head_count, top_count, BLOCK, 2 * head_size)
    for turn in range(top_count):
        parts.append(tile_partial(query_blocks, fetched[:, :, turn], scaling))
    result = merge_parts(parts)
    result = (
        result.transpose(0, 2, 1, 3)
        .reshape(qblocks * BLOCK, head_count * head_size)
        .astype(jnp.bfloat16)
    )
    return lax.all_to_all(result, ("heads", "sub"), split_axis=0, concat_axis=1, tiled=True)


def body(queries, new_keys, new_values, cache_keys, cache_values, selection):
    qblocks, head_count, top_count = selection.shape
    blocks_total = cache_keys.shape[0] // BLOCK * lax.axis_size("seq")
    if blocks_total == top_count and qblocks == 1:
        return dense_body(queries, new_keys, new_values, cache_keys, cache_values)
    return general_body(queries, new_keys, new_values, cache_keys, cache_values, selection)


def solution(mesh):
    in_specs = (
        P(("groups", "seq", "heads", "sub"), None),
        P(("groups", "seq", "heads", "sub"), None),
        P(("groups", "seq", "heads", "sub"), None),
        P(("groups", "seq"), ("heads", "sub")),
        P(("groups", "seq"), ("heads", "sub")),
        P(("groups", "seq"), ("heads", "sub"), None),
    )
    out_specs = P(("groups", "seq", "heads", "sub"), None)
    return jax.shard_map(body, mesh=mesh, in_specs=in_specs, out_specs=out_specs, check_vma=False)
```
